32 devices in a mesh: seq: 8 (over y, x, core), str: 4 (over z).
Axes of the slice: x: 2, y: 2, z: 4, core: 2. Of those that a mesh axis runs over, the one named last changes fastest.
Arguments:
- hidden: bfloat16 [4, 2048, 960], P('str', 'seq'), may hold values from -6 to 6
- lengths: int32 [4, 5], P('str'), may hold values from 1 to 768, 2048 in all within a row
- depth: int32 [4, 2048], P('str', 'seq'), may hold values from 1 to 3
- cotangent: float32 [4, 2048, 960], P('str', 'seq'), may hold values from -6 to 6
- norm1_gain: float32 [960], replicated, may hold values from 0.5 to 1.5
- w_query: bfloat16 [960, 960], replicated, may hold values from -0.1875 to 0.1875
- w_key: bfloat16 [960, 320], replicated, may hold values from -0.1875 to 0.1875
- w_value: bfloat16 [960, 320], replicated, may hold values from -0.1875 to 0.1875
- w_out: bfloat16 [960, 960], replicated, may hold values from -0.5 to 0.5
- norm2_gain: float32 [960], replicated, may hold values from 0.5 to 1.5
- w_gate: bfloat16 [960, 2560], replicated, may hold values from -0.1875 to 0.1875
- w_up: bfloat16 [960, 2560], replicated, may hold values from -0.1875 to 0.1875
- w_down: bfloat16 [2560, 960], replicated, may hold values from -0.125 to 0.125
- router: bfloat16 [3, 960], replicated, may hold values from -0.1875 to 0.1875
Outputs:
- mixed: bfloat16 [4, 2048, 960], P('str', 'seq')
- grad_hidden: float32 [4, 2048, 960], P('str', 'seq')
- grad_norm1_gain: float32 [960], P('str')
- grad_w_query: float32 [960, 960], P('str')
- grad_w_key: float32 [960, 320], P('str')
- grad_w_value: float32 [960, 320], P('str')
- grad_w_out: float32 [960, 960], P('str')
- grad_norm2_gain: float32 [960], P('str')
- grad_w_gate: float32 [960, 2560], P('str')
- grad_w_up: float32 [960, 2560], P('str')
- grad_w_down: float32 [2560, 960], P('str')
- grad_router: float32 [3, 960], P(None, 'str')
The draws below stay inside these ranges and needn't reach their ends.
Inputs may be any that keep to these rules, and one draw needn't show every extreme that they name: `lengths`: each row sums to 2048 and holds one entry of exactly 768.
All inputs are finite; a program needn't handle non-finite values.
Results may differ from the reference program's by a relative error of at most 0.025.
Values may be sent and summed in bfloat16 or wider, within the bound.
No kernel may reach another device: no remote copies, remote signals or barrier semaphores. Data moves between devices by JAX's collectives and lax.ppermute only.
A program may use at most 192 MiB of HBM per device.

```python
import math
import jax
import jax.numpy as jnp
import numpy as np
from jax import lax

D = 960
QH = 15
KVH = 5
HD = 64
FF = 2560
R = 3
KVD = 320
DOCMAX = 768
SEQLEN = 2048
STREAMS = 4
NDOC = 5


def place_ends(array, key, smallest, largest):
    longest = array.shape.index(max(array.shape))
    spots = []
    for shift in (0, 1):
        where = [jax.random.randint(jax.random.fold_in(key, axis), (), 0, length) for axis, length in enumerate(array.shape)]
        where[longest] = (where[longest] + shift) % array.shape[longest]
        spots.append(tuple(where))
    return array.at[spots[0]].set(smallest).at[spots[1]].set(largest)


def shard_levels(rng, extent, cuts, smallest, high):
    def one(dim, blocks):
        heights = jax.random.uniform(jax.random.fold_in(jax.random.fold_in(rng, 6), dim), (blocks,), jnp.float32, smallest / len(cuts), high / len(cuts))
        return jnp.repeat(jnp.exp(heights), extent[dim] // blocks).reshape((-1,) + (1,) * (len(extent) - dim - 1))

    level = one(*cuts[0])
    for cut in cuts[1:]:
        level = level * one(*cut)
    return level


def profile(number_of, total, most, skew):
    portions = [(1 << 20) // math.isqrt(grade ** skew) + 1 for grade in range(2, number_of + 1)]
    spare, holding = total - most - (number_of - 1), [1] * (number_of - 1)
    while spare > 0:
        candidates = [i for i in range(number_of - 1) if holding[i] < most]
        mass, remaining = sum([portions[i] for i in candidates]), spare
        for i in candidates:
            addition = min(most - holding[i], max(1, remaining * portions[i] // mass), spare)
            holding[i] = holding[i] + addition
            spare = spare - addition
    return np.array([most] + holding)


def uneven(stream_key, count, total, limit, slope):
    if count == 2:
        one = jax.random.randint(stream_key, (), max(1, total - limit), min(limit, total - 1) + 1)
        return jnp.stack([one, total - one])
    sizes = jnp.asarray(profile(count, total, limit, slope), jnp.int32)
    twos = (count - 1) // 2
    giver, sink = sizes[1:1 + 2 * twos:2], sizes[2:2 + 2 * twos:2]
    margin = jnp.minimum(giver - 1, limit - sink)
    passed = jax.random.randint(jax.random.fold_in(stream_key, 1), (twos,), 0, 1 << 20) % (margin + 1)
    sizes = sizes.at[1:1 + 2 * twos:2].set(giver - passed).at[2:2 + 2 * twos:2].set(sink + passed)
    return sizes[jax.random.permutation(jax.random.fold_in(stream_key, 2), count)]


def scatter_about(key, extent, spread, most, cuts=(), held_as=jnp.bfloat16):
    array = jax.random.normal(key, extent, jnp.float32) * spread
    if len(cuts) > 0:
        array = shard_levels(key, extent, cuts, -0.22, 0.18) * array
    return jnp.clip(array, min=-most, max=most).astype(held_as)


def setup_inputs(seed: int = 0) -> dict:
    key_of = jax.random.split(jax.random.key(seed), 15)
    hidden = scatter_about(key_of[0], (STREAMS, SEQLEN, D), 1.0, 6.0, ((0, 4), (1, 8)))
    lengths = jax.vmap(lambda own: uneven(own, NDOC, SEQLEN, DOCMAX, 2))(jax.random.split(key_of[1], STREAMS)).reshape((STREAMS, NDOC)).astype(jnp.int32)
    depth = place_ends(jax.random.randint(key_of[2], (STREAMS, SEQLEN), 1, R + 1), jax.random.fold_in(key_of[2], 1), 1, R).astype(jnp.int32)
    cotangent = scatter_about(key_of[3], (STREAMS, SEQLEN, D), 1.0, 6.0, ((0, 4), (1, 8)), jnp.float32)
    norm1_gain = jnp.clip(1.0 + 0.1 * jax.random.normal(key_of[4], (D,), jnp.float32), 0.5, 1.5)
    w_query = scatter_about(key_of[5], (D, D), D ** -0.5, 0.1875)
    w_key = scatter_about(key_of[6], (D, KVD), D ** -0.5, 0.1875)
    w_value = scatter_about(key_of[7], (D, KVD), D ** -0.5, 0.1875)
    w_out = scatter_about(key_of[8], (D, D), (D // 8) ** -0.5, 0.5)
    norm2_gain = jnp.clip(1.0 + 0.1 * jax.random.normal(key_of[9], (D,), jnp.float32), 0.5, 1.5)
    w_gate = scatter_about(key_of[10], (D, FF), D ** -0.5, 0.1875)
    w_up = scatter_about(key_of[11], (D, FF), D ** -0.5, 0.1875)
    w_down = scatter_about(key_of[12], (FF, D), FF ** -0.5, 0.125)
    router = scatter_about(key_of[13], (R, D), D ** -0.5, 0.1875)
    return dict(hidden=hidden, lengths=lengths, depth=depth, cotangent=cotangent, norm1_gain=norm1_gain, w_query=w_query, w_key=w_key, w_value=w_value, w_out=w_out, norm2_gain=norm2_gain, w_gate=w_gate, w_up=w_up, w_down=w_down, router=router)


@jax.custom_vjp
def low(v):
    return lax.optimization_barrier(v.astype(jnp.bfloat16)).astype(jnp.float32)

@jax.custom_vjp
def low_back(v):
    return v

def low_keep(v):
    return (low(v), None)

def low_pass(kept, grad):
    return (grad,)

def back_keep(v):
    return (v, None)

def back_low(kept, grad):
    return (low(grad),)
low.defvjp(low_keep, low_pass)
low_back.defvjp(back_keep, back_low)
EPSILON = 1e-05

def matmul(left, right):
    return jnp.dot(left, right, preferred_element_type=jnp.float32, precision=lax.Precision.HIGHEST)

def rms_norm(values, gain):
    inverse = lax.rsqrt(lax.optimization_barrier(jnp.mean(values * values, axis=-1, keepdims=True)) + EPSILON)
    return values * inverse * gain

def rotate(values, cosine_tab, sine_tab):
    half = values.shape[-1] // 2
    first = values[..., :half]
    second = values[..., half:]
    return jnp.concatenate([first * cosine_tab - second * sine_tab, second * cosine_tab + first * sine_tab], -1)

def doc_tables(positions, doc_lengths):
    ends = jnp.cumsum(doc_lengths, dtype=jnp.int32)
    after = positions[:, None] >= ends[None, :]
    doc_index = lax.optimization_barrier(jnp.sum(after.astype(jnp.int32), axis=1, dtype=jnp.int32))
    offset = lax.optimization_barrier(jnp.sum(jnp.where(after, doc_lengths[None, :], 0), axis=1, dtype=jnp.int32))
    return (doc_index, positions - offset)

def stream_forward(state, params, doc_lengths, depth_row):
    gain1, w_query, w_key, w_value, w_out, gain2, w_gate, w_up, w_down, router_rows = params
    length = state.shape[0]
    positions = jnp.arange(length, dtype=jnp.int32)
    doc_index, place = doc_tables(positions, doc_lengths)
    half = HD // 2
    freqs = jnp.exp(-math.log(10000.0) * 2.0 * jnp.arange(half, dtype=jnp.float32) / HD)
    angles = place.astype(jnp.float32)[:, None, None] * freqs[None, None, :]
    cosine_tab = jnp.cos(angles)
    sine_tab = jnp.sin(angles)
    group = QH // KVH
    block_rows = math.gcd(length, 512)
    blocks = length // block_rows
    starts = (jnp.arange(blocks, dtype=jnp.int32) * block_rows).astype(jnp.int32)
    scale = HD ** (-0.5)
    for level in range(R):
        active = depth_row > level
        normed = low(rms_norm(state, gain1))
        query_pre = low_back(matmul(normed, w_query))
        key_pre = low_back(matmul(normed, w_key))
        values_all = low_back(low(matmul(normed, w_value))).reshape(length, KVH, HD)
        queries = low(rotate(query_pre.reshape(length, QH, HD), cosine_tab, sine_tab))
        queries = queries.reshape(blocks, block_rows, KVH, group, HD)
        keys_all = low(rotate(key_pre.reshape(length, KVH, HD), cosine_tab, sine_tab))

        def one_block(inputs, keys_all=keys_all, values_all=values_all, active=active):
            query_blk, start = inputs
            query_pos = start + jnp.arange(block_rows, dtype=jnp.int32)
            query_doc = lax.dynamic_slice_in_dim(doc_index, start, block_rows)
            allowed = (doc_index[None, :] == query_doc[:, None]) & (positions[None, :] <= query_pos[:, None])
            allowed = allowed & (active[None, :] | (positions[None, :] == query_pos[:, None]))
            scores = jnp.einsum('qkgd,tkd->kgqt', query_blk, keys_all, precision=lax.Precision.HIGHEST) * scale
            scores = low_back(scores)
            scores = jnp.where(allowed[None, None], scores, -1e+30)
            probs = low(jax.nn.softmax(scores, axis=-1))
            return jnp.einsum('kgqt,tkd->qkgd', probs, values_all, precision=lax.Precision.HIGHEST)
        attended = lax.map(jax.checkpoint(one_block), (queries, starts)).reshape(length, D)
        attended = low_back(low(attended))
        attn_out = low_back(matmul(attended, w_out))
        mid_state = state + attn_out
        normed2 = low(rms_norm(mid_state, gain2))
        gate_pre = low_back(matmul(normed2, w_gate))
        up_pre = low_back(matmul(normed2, w_up))
        hidden_act = low(jax.nn.silu(gate_pre) * up_pre)
        ffn_out = low_back(matmul(hidden_act, w_down))
        gate_prob = jax.nn.sigmoid(matmul(state, router_rows[level]))
        state = state + (active.astype(jnp.float32) * gate_prob)[:, None] * (attn_out + ffn_out)
    return state

def reference(hidden, lengths, depth, cotangent, norm1_gain, w_query, w_key, w_value, w_out, norm2_gain, w_gate, w_up, w_down, router):
    params = (norm1_gain.astype(jnp.float32), w_query.astype(jnp.float32), w_key.astype(jnp.float32), w_value.astype(jnp.float32), w_out.astype(jnp.float32), norm2_gain.astype(jnp.float32), w_gate.astype(jnp.float32), w_up.astype(jnp.float32), w_down.astype(jnp.float32), router.astype(jnp.float32))

    def one_stream(totals, item):
        state, doc_lengths, depth_row, grad_out = item
        result, pullback = jax.vjp(lambda inputs, weights: stream_forward(inputs, weights, doc_lengths, depth_row), state.astype(jnp.float32), params)
        grad_in, grad_params = pullback(grad_out.astype(jnp.float32))
        totals = jax.tree.map(jnp.add, totals, grad_params)
        return (totals, (result.astype(jnp.bfloat16), grad_in))
    zeros = jax.tree.map(jnp.zeros_like, params)
    totals, (mixed, grad_hidden) = lax.scan(one_stream, zeros, (hidden, lengths, depth, cotangent))
    return (mixed, grad_hidden, totals[0], totals[1], totals[2], totals[3], totals[4], totals[5], totals[6], totals[7], totals[8], totals[9])
```

```python
import math

import jax
import jax.numpy as jnp
from jax import lax
from jax.sharding import PartitionSpec as P

HD = 64
R = 3
REACH = 3


EPSILON = 1e-05


def rms_forward(values, gain):
    inverse = lax.rsqrt(jnp.mean(values * values, axis=-1, keepdims=True) + EPSILON)
    return (values * inverse * gain, inverse)


def rms_backward(values, inverse, gain, grad_out):
    scaled = grad_out * gain
    grad_gain = jnp.sum(grad_out * values * inverse, axis=0)
    grad_in = inverse * scaled - values * inverse * inverse * inverse * jnp.mean(
        scaled * values, axis=-1, keepdims=True
    )
    return (grad_in, grad_gain)


def rotate(values, cosine_tab, sine_tab):
    half = values.shape[-1] // 2
    first = values[..., :half]
    second = values[..., half:]
    return jnp.concatenate(
        [first * cosine_tab - second * sine_tab, second * cosine_tab + first * sine_tab], -1
    )


def unrotate(grads, cosine_tab, sine_tab):
    half = grads.shape[-1] // 2
    first = grads[..., :half]
    second = grads[..., half:]
    return jnp.concatenate(
        [first * cosine_tab + second * sine_tab, second * cosine_tab - first * sine_tab], -1
    )


def doc_tables(positions, doc_lengths):
    ends = jnp.cumsum(doc_lengths, dtype=jnp.int32)
    after = positions[:, None] >= ends[None, :]
    doc_index = jnp.sum(after.astype(jnp.int32), axis=1, dtype=jnp.int32)
    offset = jnp.sum(jnp.where(after, doc_lengths[None, :], 0), axis=1, dtype=jnp.int32)
    return (doc_index, positions - offset)


def head_scores(query_grp, key_grp, allowed):
    scores = jnp.einsum(
        "qgd,td->gqt", query_grp, key_grp, preferred_element_type=jnp.float32
    ) * HD ** (-0.5)
    return jnp.where(allowed[None], scores, -1e30)


def attend_head(query_grp, key_grp, value_grp, allowed):
    scores = head_scores(query_grp, key_grp, allowed)
    peak = jnp.max(scores, axis=-1, keepdims=True)
    weights = jnp.exp(scores - peak)
    total = jnp.sum(weights, axis=-1, keepdims=True)
    probs = (weights / total).astype(jnp.bfloat16)
    output = jnp.einsum("gqt,td->qgd", probs, value_grp, preferred_element_type=jnp.float32)
    return (output, peak[..., 0] + jnp.log(total[..., 0]))


def attend_back(query_grp, key_grp, value_grp, allowed, log_total, grad_out):
    scores = head_scores(query_grp, key_grp, allowed)
    probs_full = jnp.exp(scores - log_total[..., None])
    probs = probs_full.astype(jnp.bfloat16)
    grad_probs = jnp.einsum("qgd,td->gqt", grad_out, value_grp, preferred_element_type=jnp.float32)
    grad_value = jnp.einsum("gqt,qgd->td", probs, grad_out, preferred_element_type=jnp.float32)
    delta = jnp.sum(probs_full * grad_probs, axis=-1, keepdims=True)
    grad_scores = (probs_full * (grad_probs - delta)).astype(jnp.bfloat16)
    grad_query = jnp.einsum(
        "gqt,td->qgd", grad_scores, key_grp, preferred_element_type=jnp.float32
    ) * HD ** (-0.5)
    grad_key = jnp.einsum(
        "gqt,qgd->td", grad_scores, query_grp, preferred_element_type=jnp.float32
    ) * HD ** (-0.5)
    return (grad_query, grad_key, grad_value)


def stack_heads(queries, keys_all, values_all):
    rows = queries.shape[0]
    kv_heads = keys_all.shape[1] // HD
    query_stack = queries.reshape(rows, kv_heads, -1, HD).transpose(1, 0, 2, 3)
    key_stack = keys_all.reshape(-1, kv_heads, HD).transpose(1, 0, 2)
    value_stack = values_all.reshape(-1, kv_heads, HD).transpose(1, 0, 2)
    return (query_stack, key_stack, value_stack)


def attention_forward(queries, keys_all, values_all, allowed):
    rows = queries.shape[0]
    stacks = stack_heads(queries, keys_all, values_all)
    outputs, log_total = lax.map(
        lambda group: attend_head(group[0], group[1], group[2], allowed), stacks
    )
    return (outputs.transpose(1, 0, 2, 3).reshape(rows, -1), log_total)


def attention_backward(queries, keys_all, values_all, allowed, log_total, grad_out):
    rows = queries.shape[0]
    kv_heads = keys_all.shape[1] // HD
    query_stack, key_stack, value_stack = stack_heads(queries, keys_all, values_all)
    grad_stack = grad_out.reshape(rows, kv_heads, -1, HD).transpose(1, 0, 2, 3)
    grad_query, grad_key, grad_value = lax.map(
        lambda group: attend_back(group[0], group[1], group[2], allowed, group[3], group[4]),
        (query_stack, key_stack, value_stack, log_total, grad_stack),
    )
    grad_query = grad_query.transpose(1, 0, 2, 3).reshape(rows, -1)
    grad_key = grad_key.transpose(1, 0, 2).reshape(-1, keys_all.shape[1])
    grad_value = grad_value.transpose(1, 0, 2).reshape(-1, keys_all.shape[1])
    return (grad_query, grad_key, grad_value)


def swap(block, mask):
    devices = range(lax.axis_size("seq"))
    return lax.ppermute(block, "seq", [(i, i ^ mask) for i in devices])


def moved(block, targets):
    devices = range(lax.axis_size("seq"))
    return lax.ppermute(
        block, "seq", [(i, t) for i, t in enumerate(targets) if t in devices]
    )


def halo(block):
    devices = range(lax.axis_size("seq"))
    even = lax.axis_index("seq") % 2 == 0
    two = moved(block, [i + 2 for i in devices])
    mixed = moved(block, [i + 1 if i % 2 == 0 else i + 3 for i in devices])
    across = swap(two, 1)
    return (jnp.where(even, mixed, across), two, jnp.where(even, across, mixed))


def halo_back(third, second, first):
    devices = range(lax.axis_size("seq"))
    even = lax.axis_index("seq") % 2 == 0
    across = swap(jnp.where(even, first, third).astype(jnp.bfloat16), 1)
    mixed = moved(
        jnp.where(even, third, first).astype(jnp.bfloat16),
        [i - 1 if i % 2 == 1 else i - 3 for i in devices],
    )
    both = (second + across.astype(jnp.float32)).astype(jnp.bfloat16)
    two = moved(both, [i - 2 for i in devices])
    return two.astype(jnp.float32) + mixed.astype(jnp.float32)


def bit_orders():
    devices = lax.axis_size("seq")
    rest = [1 << b for b in range(1, devices.bit_length() - 1)]
    half = len(rest) // 2
    return ([1] + rest, [1] + rest[half:] + rest[:half])


def relative(index, order):
    piece = jnp.zeros_like(index)
    for place, mask in enumerate(reversed(order)):
        piece = piece + ((index >> place) & 1) * mask
    return piece


def slot_rows(width):
    devices, streams = (lax.axis_size("seq"), lax.axis_size("str"))
    share = width // streams
    slots = -(-share // devices)
    return (share, -(-slots // 8) * 8)


def one_hot(rows, columns):
    return (rows[:, None] == columns[None, :]).astype(jnp.bfloat16)


def row_spread(width, order):
    devices, streams = (lax.axis_size("seq"), lax.axis_size("str"))
    share, slots = slot_rows(width)
    index = jnp.arange(devices * streams * slots, dtype=jnp.int32)
    slot = index % slots
    stream = (lax.axis_index("str") + (index // slots) % streams) % streams
    piece = relative(index // (slots * streams), order) ^ lax.axis_index("seq")
    inside = piece * slots + slot
    target = jnp.where(inside < share, stream * share + inside, -1)
    return one_hot(jnp.arange(width, dtype=jnp.int32), target)


def row_gather(width, order):
    devices = lax.axis_size("seq")
    share, slots = slot_rows(width)
    index = jnp.arange(devices * slots, dtype=jnp.int32)
    piece = relative(index // slots, order) ^ lax.axis_index("seq")
    return one_hot(jnp.arange(share, dtype=jnp.int32), piece * slots + index % slots)


def column_spread(width, order):
    devices = lax.axis_size("seq")
    used = -(-width // devices)
    lanes = -(-used // 128) * 128
    index = jnp.arange(devices * lanes, dtype=jnp.int32)
    piece = relative(index // lanes, order) ^ lax.axis_index("seq")
    slot = index % lanes
    target = jnp.where(slot < used, piece * used + slot, -1)
    return one_hot(jnp.arange(width, dtype=jnp.int32), target)


def low_dot(left, right):
    return jnp.dot(left, right, preferred_element_type=jnp.float32).astype(jnp.bfloat16)


def outer(left, right):
    return jnp.einsum("tm,tn->mn", left, right, preferred_element_type=jnp.float32)


def added(*terms):
    total = terms[0].astype(jnp.float32)
    for term in terms[1:]:
        total = total + term.astype(jnp.float32)
    return total.astype(jnp.bfloat16)


def reduce_rows(left, right, order):
    half = left.shape[1] // 2
    sent = outer(left[:, half:], right).astype(jnp.bfloat16)
    part = added(outer(left[:, :half], right), swap(sent, order[0]))
    for mask in order[1:]:
        half = part.shape[0] // 2
        part = added(part[:half], swap(part[half:], mask))
    streams = lax.axis_size("str")
    slots = part.shape[0] // streams
    terms = [part[:slots]]
    for distance in range(1, streams):
        route = [(i, (i + distance) % streams) for i in range(streams)]
        terms.append(
            lax.ppermute(part[distance * slots : (distance + 1) * slots], "str", route)
        )
    return added(*terms)


def collect_rows(part, order, width):
    for mask in reversed(order):
        part = jnp.concatenate([part, swap(part, mask)], 0)
    return jnp.dot(row_gather(width, order), part, preferred_element_type=jnp.float32)


def reduce_columns(left, right, order):
    half = right.shape[1] // 2
    sent = outer(left, right[:, half:]).astype(jnp.bfloat16)
    part = added(outer(left, right[:, :half]), swap(sent, order[0]))
    streams = lax.axis_size("str")
    here = lax.axis_index("str")
    route = [(i, (i + 1) % streams) for i in range(streams)]
    part = part.reshape(streams, -1, part.shape[1])

    def block(back):
        return lax.dynamic_index_in_dim(part, (here - back) % streams, 0, keepdims=False)

    running = block(1)
    for step in range(streams - 1):
        running = added(lax.ppermute(running, "str", route), block(step + 2))
    part = running
    for mask in order[1:]:
        half = part.shape[1] // 2
        part = added(part[:, :half], swap(part[:, half:], mask))
    return part


def collect_columns(part, order, width):
    for mask in reversed(order):
        part = jnp.concatenate([part, swap(part, mask)], 1)
    return jnp.einsum(
        "fm,dm->fd", part, column_spread(width, order), preferred_element_type=jnp.float32
    )


def stacked(values):
    return jnp.concatenate(values, 0)


def per_device(
    hidden,
    lengths,
    depth,
    cotangent,
    norm1_gain,
    w_query,
    w_key,
    w_value,
    w_out,
    norm2_gain,
    w_gate,
    w_up,
    w_down,
    router,
):
    rows, width = hidden.shape[1:]
    key_width = w_key.shape[1]
    seq_index = lax.axis_index("seq")
    local_pos = seq_index * rows + jnp.arange(rows, dtype=jnp.int32)
    key_pos = (seq_index - REACH) * rows + jnp.arange((REACH + 1) * rows, dtype=jnp.int32)
    doc_lengths = lengths[0]
    query_doc, place = doc_tables(local_pos, doc_lengths)
    key_doc, unused_place = doc_tables(key_pos, doc_lengths)
    base_mask = (
        (key_pos[None, :] >= 0)
        & (key_pos[None, :] <= local_pos[:, None])
        & (key_doc[None, :] == query_doc[:, None])
    )
    own_key = key_pos[None, :] == local_pos[:, None]
    half = HD // 2
    freqs = jnp.exp(-math.log(10000.0) * 2.0 * jnp.arange(half, dtype=jnp.float32) / HD)
    angles = place.astype(jnp.float32)[:, None, None] * freqs[None, None, :]
    cosine_tab = jnp.cos(angles)
    sine_tab = jnp.sin(angles)
    depth_row = depth[0]
    depth_all = jnp.concatenate([*halo(depth_row), depth_row], 0)
    router_rows = router.astype(jnp.float32)
    order_a, order_b = bit_orders()
    spread_a = row_spread(width, order_a)
    spread_b = row_spread(width, order_b)
    state = hidden[0].astype(jnp.float32)
    saved = []
    for level in range(R):
        normed, inverse1 = rms_forward(state, norm1_gain)
        normed_low = normed.astype(jnp.bfloat16)
        key_pre = jnp.dot(normed_low, w_key, preferred_element_type=jnp.float32)
        value_low = low_dot(normed_low, w_value)
        key_low = (
            rotate(key_pre.reshape(rows, -1, HD), cosine_tab, sine_tab)
            .reshape(rows, -1)
            .astype(jnp.bfloat16)
        )
        local_pair = jnp.concatenate([key_low, value_low], 1)
        pair = jnp.concatenate([*halo(local_pair), local_pair], 0)
        query_pre = jnp.dot(normed_low, w_query, preferred_element_type=jnp.float32)
        query_low = (
            rotate(query_pre.reshape(rows, -1, HD), cosine_tab, sine_tab)
            .reshape(rows, -1)
            .astype(jnp.bfloat16)
        )
        keys_all = pair[:, :key_width]
        values_all = pair[:, key_width:]
        allowed = base_mask & ((depth_all > level)[None, :] | own_key)
        attended, log_total = attention_forward(query_low, keys_all, values_all, allowed)
        attended_low = attended.astype(jnp.bfloat16)
        attn_out = jnp.dot(attended_low, w_out, preferred_element_type=jnp.float32)
        mid_state = state + attn_out
        normed2, inverse2 = rms_forward(mid_state, norm2_gain)
        normed2_low = normed2.astype(jnp.bfloat16)
        gate_pre = jnp.dot(normed2_low, w_gate, preferred_element_type=jnp.float32)
        up_pre = jnp.dot(normed2_low, w_up, preferred_element_type=jnp.float32)
        hidden_act = (jax.nn.silu(gate_pre) * up_pre).astype(jnp.bfloat16)
        ffn_out = jnp.dot(hidden_act, w_down, preferred_element_type=jnp.float32)
        gate_prob = jax.nn.sigmoid(
            jnp.dot(state, router_rows[level], precision=lax.Precision.HIGHEST)
        )
        active = (depth_row > level).astype(jnp.float32)
        both = attn_out + ffn_out
        saved.append(
            (
                state,
                inverse1,
                normed_low,
                query_low,
                keys_all,
                values_all,
                allowed,
                log_total,
                attended_low,
                mid_state,
                inverse2,
                normed2_low,
                gate_pre,
                up_pre,
                hidden_act,
                both,
                gate_prob,
                active,
            )
        )
        state = state + (active * gate_prob)[:, None] * both
    mixed = state.astype(jnp.bfloat16)[None]
    grad_state = cotangent[0]
    normed_spread = stacked([low_dot(item[2], spread_a) for item in saved])
    attended_spread = stacked([low_dot(item[8], spread_b) for item in saved])
    normed2_low = stacked([item[11] for item in saved])
    gate_spread = low_dot(normed2_low, spread_a)
    up_spread = low_dot(normed2_low, spread_b)
    hidden_cat = stacked([item[14] for item in saved])
    column_order = order_a
    spread_c = column_spread(width, column_order)
    factors = [[None] * R for kind in range(5)]
    down_part = None
    for level in range(R - 1, -1, -1):
        (
            state,
            inverse1,
            normed_low,
            query_low,
            keys_all,
            values_all,
            allowed,
            log_total,
            attended_low,
            mid_state,
            inverse2,
            unused_low,
            gate_pre,
            up_pre,
            hidden_act,
            both,
            gate_prob,
            active,
        ) = saved[level]
        grad_branch = (active * gate_prob)[:, None] * grad_state
        grad_logit = jnp.sum(grad_state * both, axis=-1) * active * gate_prob * (1.0 - gate_prob)
        grad_next = grad_state + grad_logit[:, None] * router_rows[level][None, :]
        grad_ffn = grad_branch.astype(jnp.bfloat16)
        factors[0][level] = low_dot(grad_ffn, spread_c)
        if level == 0:
            down_part = reduce_columns(hidden_cat, stacked(factors[0]), column_order)
        grad_act = jnp.einsum("td,fd->tf", grad_ffn, w_down, preferred_element_type=jnp.float32)
        sigma = jax.nn.sigmoid(gate_pre)
        grad_gate = (grad_act * up_pre * sigma * (1.0 + gate_pre * (1.0 - sigma))).astype(
            jnp.bfloat16
        )
        grad_up_pre = (grad_act * gate_pre * sigma).astype(jnp.bfloat16)
        factors[1][level] = grad_gate
        factors[2][level] = grad_up_pre
        if level == 0:
            gate_part = reduce_rows(gate_spread, stacked(factors[1]), order_a)
            up_part = reduce_rows(up_spread, stacked(factors[2]), order_b)
        grad_normed2 = jnp.einsum(
            "tf,df->td", grad_gate, w_gate, preferred_element_type=jnp.float32
        )
        grad_normed2 = grad_normed2 + jnp.einsum(
            "tf,df->td", grad_up_pre, w_up, preferred_element_type=jnp.float32
        )
        grad_mid, unused_gain = rms_backward(mid_state, inverse2, norm2_gain, grad_normed2)
        grad_next = grad_next + grad_mid
        grad_attn = (grad_branch + grad_mid).astype(jnp.bfloat16)
        factors[3][level] = grad_attn
        if level == 0:
            out_part = reduce_rows(attended_spread, stacked(factors[3]), order_b)
        grad_attended = jnp.einsum(
            "te,de->td", grad_attn, w_out, preferred_element_type=jnp.float32
        ).astype(jnp.bfloat16)
        grad_query, grad_keys, grad_values = attention_backward(
            query_low, keys_all, values_all, allowed, log_total, grad_attended
        )
        grad_pair = jnp.concatenate([grad_keys, grad_values], 1)
        local_pair = grad_pair[REACH * rows :] + halo_back(
            grad_pair[:rows], grad_pair[rows : 2 * rows], grad_pair[2 * rows : 3 * rows]
        )
        grad_query_pre = (
            unrotate(grad_query.reshape(rows, -1, HD), cosine_tab, sine_tab)
            .reshape(rows, -1)
            .astype(jnp.bfloat16)
        )
        grad_key_pre = (
            unrotate(local_pair[:, :key_width].reshape(rows, -1, HD), cosine_tab, sine_tab)
            .reshape(rows, -1)
            .astype(jnp.bfloat16)
        )
        grad_value_pre = local_pair[:, key_width:].astype(jnp.bfloat16)
        router_term = (grad_logit / inverse1[:, 0])[:, None] * (
            jnp.arange(R)[None, :] == level
        ).astype(jnp.float32)
        factors[4][level] = jnp.concatenate(
            [grad_query_pre, grad_key_pre, grad_value_pre, router_term.astype(jnp.bfloat16)], 1
        )
        grad_normed = jnp.einsum(
            "te,de->td", grad_query_pre, w_query, preferred_element_type=jnp.float32
        )
        grad_normed = grad_normed + jnp.einsum(
            "te,de->td", grad_key_pre, w_key, preferred_element_type=jnp.float32
        )
        grad_normed = grad_normed + jnp.einsum(
            "te,de->td", grad_value_pre, w_value, preferred_element_type=jnp.float32
        )
        grad_input, unused_gain = rms_backward(state, inverse1, norm1_gain, grad_normed)
        grad_state = grad_next + grad_input
    front_part = reduce_rows(normed_spread, stacked(factors[4]), order_a)
    down_sum = collect_columns(down_part, column_order, width)
    gate_sum = collect_rows(gate_part, order_a, width)
    up_sum = collect_rows(up_part, order_b, width)
    out_sum = collect_rows(out_part, order_b, width)
    front_sum = collect_rows(front_part, order_a, width)
    share = gate_sum.shape[0]
    first = lax.axis_index("str") * share

    def mine(table):
        return lax.dynamic_slice_in_dim(table, first, share, 0)

    gain1, gain2 = (mine(norm1_gain), mine(norm2_gain))
    query_sum = front_sum[:, :width]
    key_sum = front_sum[:, width : width + key_width]
    value_sum = front_sum[:, width + key_width : width + 2 * key_width]
    router_sum = (front_sum[:, width + 2 * key_width :] / gain1[:, None]).T

    def row_dots(weights, sums):
        return jnp.sum(mine(weights).astype(jnp.float32) * sums, axis=1)

    gain1_sum = (
        row_dots(w_query, query_sum) + row_dots(w_key, key_sum) + row_dots(w_value, value_sum)
    ) / gain1
    gain2_sum = (row_dots(w_gate, gate_sum) + row_dots(w_up, up_sum)) / gain2
    return (
        mixed,
        grad_state[None],
        gain1_sum,
        query_sum,
        key_sum,
        value_sum,
        out_sum,
        gain2_sum,
        gate_sum,
        up_sum,
        down_sum,
        router_sum,
    )


def solution(mesh):
    in_specs = (
        P("str", "seq", None),
        P("str", None),
        P("str", "seq"),
        P("str", "seq", None),
        P(),
        P(),
        P(),
        P(),
        P(),
        P(),
        P(),
        P(),
        P(),
        P(),
    )
    out_specs = (
        P("str", "seq", None),
        P("str", "seq", None),
        P("str"),
        P("str", None),
        P("str", None),
        P("str", None),
        P("str", None),
        P("str"),
        P("str", None),
        P("str", None),
        P("str", None),
        P(None, "str"),
    )
    return jax.shard_map(
        per_device, mesh=mesh, in_specs=in_specs, out_specs=out_specs, check_vma=False
    )
```

```python
import math

import jax
import jax.numpy as jnp
from jax import lax
from jax.experimental import pallas as pl
from jax.experimental.pallas import tpu as pltpu
from jax.sharding import PartitionSpec as P

HD = 64
R = 3
REACH = 3


EPSILON = 1e-05


def rms_forward(values, gain):
    inverse = lax.rsqrt(jnp.mean(values * values, axis=-1, keepdims=True) + EPSILON)
    return (values * inverse * gain, inverse)


def rms_backward(values, inverse, gain, grad_out):
    scaled = grad_out * gain
    grad_gain = jnp.sum(grad_out * values * inverse, axis=0)
    grad_in = inverse * scaled - values * inverse * inverse * inverse * jnp.mean(
        scaled * values, axis=-1, keepdims=True
    )
    return (grad_in, grad_gain)


def rotate(values, cosine_tab, sine_tab):
    heads = values.reshape(-1, 2, HD // 2, values.shape[-1])
    first, second = (heads[:, 0], heads[:, 1])
    return jnp.stack(
        [first * cosine_tab - second * sine_tab, second * cosine_tab + first * sine_tab], 1
    ).reshape(values.shape)


def unrotate(grads, cosine_tab, sine_tab):
    return rotate(grads, cosine_tab, -sine_tab)


def doc_tables(positions, doc_lengths):
    ends = jnp.cumsum(doc_lengths, dtype=jnp.int32)
    after = positions[:, None] >= ends[None, :]
    doc_index = jnp.sum(after.astype(jnp.int32), axis=1, dtype=jnp.int32)
    offset = jnp.sum(jnp.where(after, doc_lengths[None, :], 0), axis=1, dtype=jnp.int32)
    return (doc_index, positions - offset)


def tile_bias(base, tile, low_key, positions, active):
    rows = active.shape[0]
    keys = base + tile * rows + lax.broadcasted_iota(jnp.int32, (rows, positions.shape[1]), 0)
    own = keys == positions
    seen = (keys >= low_key) & (keys <= positions) & ((active > 0) | own)
    return jnp.where(seen, 0.0, -1e30)


def attend_kernel(places, low_ref, act_ref, query_ref, k0, k1, k2, k3, v0, v1, v2, v3,
                  out_ref, log_ref, bias_ref, key_ref, value_ref, top_ref, sum_ref, acc_ref):
    rows = k0.shape[1]
    heads = query_ref.shape[0] // HD
    first_tile = places[1]
    @pl.when(pl.program_id(0) == 0)
    def _():
        positions = places[0] + lax.broadcasted_iota(jnp.int32, (1, rows), 1)
        for tile in range(REACH + 1):
            @pl.when(tile >= first_tile)
            def _(tile=tile):
                bias_ref[tile] = tile_bias(places[0] - REACH * rows, tile, low_ref[...], positions,
                                           act_ref[tile * rows:(tile + 1) * rows, :])
    even = places[2] == 0
    key_ref[3] = k0[...]
    value_ref[3] = v0[...]
    key_ref[2] = jnp.where(even, k3[...], k1[...])
    value_ref[2] = jnp.where(even, v3[...], v1[...])
    key_ref[1] = k2[...]
    value_ref[1] = v2[...]
    key_ref[0] = jnp.where(even, k1[...], k3[...])
    value_ref[0] = jnp.where(even, v1[...], v3[...])
    query = query_ref[...] * jnp.bfloat16(HD ** (-0.5))
    query = jnp.concatenate([query[i * HD:(i + 1) * HD] for i in range(heads)], 1)

    def scores(tile):
        s = lax.dot_general(key_ref[tile], query, (((0,), (0,)), ((), ())), preferred_element_type=jnp.float32)
        bias = bias_ref[tile]
        return s + jnp.concatenate([bias] * heads, 1)

    s = scores(REACH)
    top = jnp.max(s, axis=0, keepdims=True)
    p = jnp.exp(s - top)
    top_ref[...] = top
    sum_ref[...] = jnp.sum(p, axis=0, keepdims=True)
    acc_ref[...] = jnp.dot(value_ref[REACH], p.astype(jnp.bfloat16), preferred_element_type=jnp.float32)

    def body(tile, carry):
        s = scores(tile)
        old = top_ref[...]
        top = jnp.maximum(old, jnp.max(s, axis=0, keepdims=True))
        p = jnp.exp(s - top)
        keep = jnp.exp(old - top)
        top_ref[...] = top
        sum_ref[...] = sum_ref[...] * keep + jnp.sum(p, axis=0, keepdims=True)
        acc_ref[...] = acc_ref[...] * keep + jnp.dot(value_ref[tile], p.astype(jnp.bfloat16), preferred_element_type=jnp.float32)
        return carry
    lax.fori_loop(first_tile, REACH, body, 0)
    total = sum_ref[...]
    out = (acc_ref[...] / total).astype(jnp.bfloat16)
    for i in range(heads):
        out_ref[i * HD:(i + 1) * HD, :] = out[:, i * rows:(i + 1) * rows]
    log_ref[0] = top_ref[...] + jnp.log(total)


def pair_specs(rows, heads):
    keys = pl.BlockSpec((HD, rows), lambda h, places: (h, 0))
    values = pl.BlockSpec((HD, rows), lambda h, places: (heads + h, 0))
    return [keys] * 4 + [values] * 4


def attend(places, low_key, active, query, pairs):
    width, rows = query.shape
    heads = pairs[0].shape[0] // (2 * HD)
    group = width // heads
    wide = group // HD * rows
    whole = lambda h, places: (0, 0)
    return pl.pallas_call(
        attend_kernel,
        out_shape=(jax.ShapeDtypeStruct((width, rows), jnp.bfloat16),
                   jax.ShapeDtypeStruct((heads, 1, wide), jnp.float32)),
        grid_spec=pltpu.PrefetchScalarGridSpec(
            num_scalar_prefetch=1, grid=(heads,),
            in_specs=[pl.BlockSpec((1, rows), whole), pl.BlockSpec((4 * rows, 1), whole),
                      pl.BlockSpec((group, rows), lambda h, places: (h, 0))] + pair_specs(rows, heads),
            out_specs=(pl.BlockSpec((group, rows), lambda h, places: (h, 0)),
                       pl.BlockSpec((1, 1, wide), lambda h, places: (h, 0, 0))),
            scratch_shapes=[pltpu.VMEM((4, rows, rows), jnp.float32),
                            pltpu.VMEM((4, HD, rows), jnp.bfloat16),
                            pltpu.VMEM((4, HD, rows), jnp.bfloat16),
                            pltpu.VMEM((1, wide), jnp.float32),
                            pltpu.VMEM((1, wide), jnp.float32),
                            pltpu.VMEM((HD, wide), jnp.float32)]),
        cost_estimate=pl.CostEstimate(flops=4 * width * rows * rows * 16, bytes_accessed=4 * width * rows * 2, transcendentals=0),
        name="attend",
    )(places, low_key, active, query, *pairs, *pairs)


def attend_back_kernel(places, low_ref, act_ref, query_ref, out_ref, grad_ref, log_ref, k0, k1, k2, k3, v0, v1, v2, v3,
                       dq_ref, own_ref, prev_ref, bias_ref, key_ref, value_ref, acc_ref):
    rows = k0.shape[1]
    heads = query_ref.shape[0] // HD
    first_tile = places[1]
    @pl.when(pl.program_id(0) == 0)
    def _():
        positions = places[0] + lax.broadcasted_iota(jnp.int32, (1, rows), 1)
        for tile in range(REACH + 1):
            @pl.when(tile >= first_tile)
            def _(tile=tile):
                bias_ref[tile] = tile_bias(places[0] - REACH * rows, tile, low_ref[...], positions,
                                           act_ref[tile * rows:(tile + 1) * rows, :])
    even = places[2] == 0
    key_ref[3] = k0[...]
    value_ref[3] = v0[...]
    key_ref[2] = jnp.where(even, k3[...], k1[...])
    value_ref[2] = jnp.where(even, v3[...], v1[...])
    key_ref[1] = k2[...]
    value_ref[1] = v2[...]
    key_ref[0] = jnp.where(even, k1[...], k3[...])
    value_ref[0] = jnp.where(even, v1[...], v3[...])
    spread = lambda x: jnp.concatenate([x[i * HD:(i + 1) * HD] for i in range(heads)], 1)
    query = spread(query_ref[...] * jnp.bfloat16(HD ** (-0.5)))
    grad = spread(grad_ref[...])
    delta = jnp.sum(grad.astype(jnp.float32) * spread(out_ref[...]).astype(jnp.float32), axis=0, keepdims=True)
    logs = log_ref[0]
    acc_ref[...] = jnp.zeros_like(acc_ref)

    def step(tile):
        s = lax.dot_general(key_ref[tile], query, (((0,), (0,)), ((), ())), preferred_element_type=jnp.float32)
        bias = bias_ref[tile]
        p = jnp.exp(s + jnp.concatenate([bias] * heads, 1) - logs)
        dp = lax.dot_general(value_ref[tile], grad, (((0,), (0,)), ((), ())), preferred_element_type=jnp.float32)
        ds = (p * (dp - delta)).astype(jnp.bfloat16)
        acc_ref[...] += jnp.dot(key_ref[tile], ds, preferred_element_type=jnp.float32)
        dk = lax.dot_general(query, ds, (((1,), (1,)), ((), ())), preferred_element_type=jnp.float32)
        dv = lax.dot_general(grad, p.astype(jnp.bfloat16), (((1,), (1,)), ((), ())), preferred_element_type=jnp.float32)
        return dk, dv

    dk, dv = step(REACH)
    own_ref[0] = dk
    own_ref[1] = dv
    prev_ref[...] = jnp.zeros_like(prev_ref)

    def body(tile, carry):
        dk, dv = step(tile)
        slot = jnp.where(even, tile, REACH - 1 - tile)
        prev_ref[slot, 0] = dk.astype(jnp.bfloat16)
        prev_ref[slot, 1] = dv.astype(jnp.bfloat16)
        return carry
    lax.fori_loop(first_tile, REACH, body, 0)
    dq = acc_ref[...] * (HD ** (-0.5))
    for i in range(heads):
        dq_ref[i * HD:(i + 1) * HD, :] = dq[:, i * rows:(i + 1) * rows]


def attend_back(places, low_key, active, query, out, grad, logs, pairs):
    width, rows = query.shape
    heads = pairs[0].shape[0] // (2 * HD)
    group = width // heads
    wide = group // HD * rows
    whole = lambda h, places: (0, 0)
    mine = pl.BlockSpec((group, rows), lambda h, places: (h, 0))
    own = pl.BlockSpec((2, HD, rows), lambda h, places: (0, h, 0))
    prev = pl.BlockSpec((REACH, 2, HD, rows), lambda h, places: (0, 0, h, 0))
    return pl.pallas_call(
        attend_back_kernel,
        out_shape=(jax.ShapeDtypeStruct((width, rows), jnp.float32),
                   jax.ShapeDtypeStruct((2, heads * HD, rows), jnp.float32),
                   jax.ShapeDtypeStruct((REACH, 2, heads * HD, rows), jnp.bfloat16)),
        grid_spec=pltpu.PrefetchScalarGridSpec(
            num_scalar_prefetch=1, grid=(heads,),
            in_specs=[pl.BlockSpec((1, rows), whole), pl.BlockSpec((4 * rows, 1), whole),
                      mine, mine, mine, pl.BlockSpec((1, 1, wide), lambda h, places: (h, 0, 0))] + pair_specs(rows, heads),
            out_specs=(mine, own, prev),
            scratch_shapes=[pltpu.VMEM((4, rows, rows), jnp.float32),
                            pltpu.VMEM((4, HD, rows), jnp.bfloat16),
                            pltpu.VMEM((4, HD, rows), jnp.bfloat16),
                            pltpu.VMEM((HD, wide), jnp.float32)]),
        cost_estimate=pl.CostEstimate(flops=10 * width * rows * rows * 16, bytes_accessed=8 * width * rows * 2, transcendentals=0),
        name="attend_back",
    )(places, low_key, active, query, out, grad, logs, *pairs, *pairs)


def swap(block, mask):
    devices = range(lax.axis_size("seq"))
    return lax.ppermute(block, "seq", [(i, i ^ mask) for i in devices])


def moved(block, targets):
    devices = range(lax.axis_size("seq"))
    return lax.ppermute(
        block, "seq", [(i, t) for i, t in enumerate(targets) if t in devices]
    )


def halo(block):
    devices = range(lax.axis_size("seq"))
    two = moved(block, [i + 2 for i in devices])
    mixed = moved(block, [i + 1 if i % 2 == 0 else i + 3 for i in devices])
    return (mixed, two, swap(two, 1))


def halo_back(mixed, second, across):
    devices = range(lax.axis_size("seq"))
    across = swap(across, 1)
    mixed = moved(mixed, [i - 1 if i % 2 == 1 else i - 3 for i in devices])
    two = moved(added(second, across), [i - 2 for i in devices])
    return two.astype(jnp.float32) + mixed.astype(jnp.float32)


def bit_orders():
    devices = lax.axis_size("seq")
    rest = [1 << b for b in range(1, devices.bit_length() - 1)]
    half = len(rest) // 2
    return ([1] + rest, [1] + rest[half:] + rest[:half])


def relative(index, order):
    piece = jnp.zeros_like(index)
    for place, mask in enumerate(reversed(order)):
        piece = piece + ((index >> place) & 1) * mask
    return piece


def slot_rows(width):
    devices, streams = (lax.axis_size("seq"), lax.axis_size("str"))
    share = width // streams
    slots = -(-share // devices)
    return (share, -(-slots // 8) * 8)


def one_hot(rows, columns):
    return (rows[:, None] == columns[None, :]).astype(jnp.bfloat16)


def row_spread(width, order):
    devices, streams = (lax.axis_size("seq"), lax.axis_size("str"))
    share, slots = slot_rows(width)
    index = jnp.arange(devices * streams * slots, dtype=jnp.int32)
    slot = index % slots
    stream = (lax.axis_index("str") + (index // slots) % streams) % streams
    piece = relative(index // (slots * streams), order) ^ lax.axis_index("seq")
    inside = piece * slots + slot
    target = jnp.where(inside < share, stream * share + inside, -1)
    return one_hot(jnp.arange(width, dtype=jnp.int32), target)


def row_gather(width, order):
    devices = lax.axis_size("seq")
    share, slots = slot_rows(width)
    index = jnp.arange(devices * slots, dtype=jnp.int32)
    piece = relative(index // slots, order) ^ lax.axis_index("seq")
    return one_hot(jnp.arange(share, dtype=jnp.int32), piece * slots + index % slots)


def column_spread(width, order):
    devices = lax.axis_size("seq")
    used = -(-width // devices)
    lanes = -(-used // 128) * 128
    index = jnp.arange(devices * lanes, dtype=jnp.int32)
    piece = relative(index // lanes, order) ^ lax.axis_index("seq")
    slot = index % lanes
    target = jnp.where(slot < used, piece * used + slot, -1)
    return one_hot(jnp.arange(width, dtype=jnp.int32), target)


def low_dot(left, right):
    return jnp.dot(left, right, preferred_element_type=jnp.float32).astype(jnp.bfloat16)


def outer(left, right):
    return jnp.einsum("tm,tn->mn", left, right, preferred_element_type=jnp.float32)


def added(*terms):
    total = terms[0].astype(jnp.float32)
    for term in terms[1:]:
        total = total + term.astype(jnp.float32)
    return total.astype(jnp.bfloat16)


def reduce_rows(left, right, order):
    half = left.shape[1] // 2
    sent = outer(left[:, half:], right).astype(jnp.bfloat16)
    part = added(outer(left[:, :half], right), swap(sent, order[0]))
    for mask in order[1:]:
        half = part.shape[0] // 2
        part = added(part[:half], swap(part[half:], mask))
    streams = lax.axis_size("str")
    slots = part.shape[0] // streams
    terms = [part[:slots]]
    for distance in range(1, streams):
        route = [(i, (i + distance) % streams) for i in range(streams)]
        terms.append(
            lax.ppermute(part[distance * slots : (distance + 1) * slots], "str", route)
        )
    return added(*terms)


def collect_rows(part, order, width):
    for mask in reversed(order):
        part = jnp.concatenate([part, swap(part, mask)], 0)
    return jnp.dot(row_gather(width, order), part, preferred_element_type=jnp.float32)


def reduce_columns(left, right, order):
    half = right.shape[1] // 2
    sent = outer(left, right[:, half:]).astype(jnp.bfloat16)
    part = added(outer(left, right[:, :half]), swap(sent, order[0]))
    streams = lax.axis_size("str")
    here = lax.axis_index("str")
    route = [(i, (i + 1) % streams) for i in range(streams)]
    part = part.reshape(streams, -1, part.shape[1])

    def block(back):
        return lax.dynamic_index_in_dim(part, (here - back) % streams, 0, keepdims=False)

    running = block(1)
    for step in range(streams - 1):
        running = added(lax.ppermute(running, "str", route), block(step + 2))
    part = running
    for mask in order[1:]:
        half = part.shape[1] // 2
        part = added(part[:, :half], swap(part[:, half:], mask))
    return part


def collect_columns(part, order, width):
    for mask in reversed(order):
        part = jnp.concatenate([part, swap(part, mask)], 1)
    return jnp.einsum(
        "fm,dm->fd", part, column_spread(width, order), preferred_element_type=jnp.float32
    )


def stacked(values):
    return jnp.concatenate(values, 0)


def per_device(
    hidden,
    lengths,
    depth,
    cotangent,
    norm1_gain,
    w_query,
    w_key,
    w_value,
    w_out,
    norm2_gain,
    w_gate,
    w_up,
    w_down,
    router,
):
    rows, width = hidden.shape[1:]
    key_width = w_key.shape[1]
    seq_index = lax.axis_index("seq")
    local_pos = seq_index * rows + jnp.arange(rows, dtype=jnp.int32)
    doc_lengths = lengths[0]
    unused_doc, place = doc_tables(local_pos, doc_lengths)
    low_key = (local_pos - place)[None, :]
    window = (seq_index - REACH) * rows
    first_tile = jnp.maximum((low_key[0, 0] - window) // rows, 0)
    even = seq_index % 2
    places = jnp.stack([seq_index * rows, first_tile, even]).astype(jnp.int32)
    half = HD // 2
    freqs = jnp.exp(-math.log(10000.0) * 2.0 * jnp.arange(half, dtype=jnp.float32) / HD)
    angles = freqs[:, None] * place.astype(jnp.float32)[None, :]
    cosine_tab = jnp.cos(angles)
    sine_tab = jnp.sin(angles)
    depth_row = depth[0]
    mixed_depth, two_depth, across_depth = halo(depth_row)
    depth_all = jnp.concatenate(
        [
            jnp.where(even == 0, mixed_depth, across_depth),
            two_depth,
            jnp.where(even == 0, across_depth, mixed_depth),
            depth_row,
        ],
        0,
    )
    router_rows = router.astype(jnp.float32)
    order_a, order_b = bit_orders()
    spread_a = row_spread(width, order_a)
    spread_b = row_spread(width, order_b)
    state = hidden[0].astype(jnp.float32)
    saved = []
    for level in range(R):
        normed, inverse1 = rms_forward(state, norm1_gain)
        normed_low = normed.astype(jnp.bfloat16)
        key_pre = jnp.dot(normed_low, w_key, preferred_element_type=jnp.float32)
        value_low = low_dot(normed_low, w_value)
        key_low = rotate(key_pre.T, cosine_tab, sine_tab).astype(jnp.bfloat16)
        local_pair = jnp.concatenate([key_low, value_low.T], 0)
        pairs = (local_pair, *halo(local_pair))
        query_pre = jnp.dot(normed_low, w_query, preferred_element_type=jnp.float32)
        query_low = rotate(query_pre.T, cosine_tab, sine_tab).astype(jnp.bfloat16)
        activity = (depth_all > level).astype(jnp.int32)[:, None]
        attended, log_total = attend(places, low_key, activity, query_low, pairs)
        attended_low = attended.T
        attn_out = jnp.dot(attended_low, w_out, preferred_element_type=jnp.float32)
        mid_state = state + attn_out
        normed2, inverse2 = rms_forward(mid_state, norm2_gain)
        normed2_low = normed2.astype(jnp.bfloat16)
        gate_pre = jnp.dot(normed2_low, w_gate, preferred_element_type=jnp.float32)
        up_pre = jnp.dot(normed2_low, w_up, preferred_element_type=jnp.float32)
        hidden_act = (jax.nn.silu(gate_pre) * up_pre).astype(jnp.bfloat16)
        ffn_out = jnp.dot(hidden_act, w_down, preferred_element_type=jnp.float32)
        gate_prob = jax.nn.sigmoid(
            jnp.dot(state, router_rows[level], precision=lax.Precision.HIGHEST)
        )
        active = (depth_row > level).astype(jnp.float32)
        both = attn_out + ffn_out
        saved.append(
            (
                state,
                inverse1,
                normed_low,
                query_low,
                pairs,
                activity,
                attended,
                log_total,
                attended_low,
                mid_state,
                inverse2,
                normed2_low,
                gate_pre,
                up_pre,
                hidden_act,
                both,
                gate_prob,
                active,
            )
        )
        state = state + (active * gate_prob)[:, None] * both
    mixed = state.astype(jnp.bfloat16)[None]
    grad_state = cotangent[0]
    normed_spread = stacked([low_dot(item[2], spread_a) for item in saved])
    attended_spread = stacked([low_dot(item[8], spread_b) for item in saved])
    normed2_low = stacked([item[11] for item in saved])
    gate_spread = low_dot(normed2_low, spread_a)
    up_spread = low_dot(normed2_low, spread_b)
    hidden_cat = stacked([item[14] for item in saved])
    column_order = order_a
    spread_c = column_spread(width, column_order)
    factors = [[None] * R for kind in range(5)]
    down_part = None
    for level in range(R - 1, -1, -1):
        (
            state,
            inverse1,
            normed_low,
            query_low,
            pairs,
            activity,
            attended,
            log_total,
            attended_low,
            mid_state,
            inverse2,
            unused_low,
            gate_pre,
            up_pre,
            hidden_act,
            both,
            gate_prob,
            active,
        ) = saved[level]
        grad_branch = (active * gate_prob)[:, None] * grad_state
        grad_logit = jnp.sum(grad_state * both, axis=-1) * active * gate_prob * (1.0 - gate_prob)
        grad_next = grad_state + grad_logit[:, None] * router_rows[level][None, :]
        grad_ffn = grad_branch.astype(jnp.bfloat16)
        factors[0][level] = low_dot(grad_ffn, spread_c)
        if level == 0:
            down_part = reduce_columns(hidden_cat, stacked(factors[0]), column_order)
        grad_act = jnp.einsum("td,fd->tf", grad_ffn, w_down, preferred_element_type=jnp.float32)
        sigma = jax.nn.sigmoid(gate_pre)
        grad_gate = (grad_act * up_pre * sigma * (1.0 + gate_pre * (1.0 - sigma))).astype(
            jnp.bfloat16
        )
        grad_up_pre = (grad_act * gate_pre * sigma).astype(jnp.bfloat16)
        factors[1][level] = grad_gate
        factors[2][level] = grad_up_pre
        if level == 0:
            gate_part = reduce_rows(gate_spread, stacked(factors[1]), order_a)
            up_part = reduce_rows(up_spread, stacked(factors[2]), order_b)
        grad_normed2 = jnp.einsum(
            "tf,df->td", grad_gate, w_gate, preferred_element_type=jnp.float32
        )
        grad_normed2 = grad_normed2 + jnp.einsum(
            "tf,df->td", grad_up_pre, w_up, preferred_element_type=jnp.float32
        )
        grad_mid, unused_gain = rms_backward(mid_state, inverse2, norm2_gain, grad_normed2)
        grad_next = grad_next + grad_mid
        grad_attn = (grad_branch + grad_mid).astype(jnp.bfloat16)
        factors[3][level] = grad_attn
        if level == 0:
            out_part = reduce_rows(attended_spread, stacked(factors[3]), order_b)
        grad_attended = jnp.einsum(
            "te,de->td", grad_attn, w_out, preferred_element_type=jnp.float32
        ).astype(jnp.bfloat16)
        grad_query, own_pair, prior = attend_back(
            places, low_key, activity, query_low, attended, grad_attended.T, log_total, pairs
        )
        prior = prior.reshape(REACH, -1, rows)
        local_pair = own_pair.reshape(-1, rows) + halo_back(prior[0], prior[1], prior[2])
        grad_query_pre = unrotate(grad_query, cosine_tab, sine_tab).astype(jnp.bfloat16).T
        grad_key_pre = (
            unrotate(local_pair[:key_width], cosine_tab, sine_tab).astype(jnp.bfloat16).T
        )
        grad_value_pre = local_pair[key_width:].astype(jnp.bfloat16).T
        router_term = (grad_logit / inverse1[:, 0])[:, None] * (
            jnp.arange(R)[None, :] == level
        ).astype(jnp.float32)
        factors[4][level] = jnp.concatenate(
            [grad_query_pre, grad_key_pre, grad_value_pre, router_term.astype(jnp.bfloat16)], 1
        )
        grad_normed = jnp.einsum(
            "te,de->td", grad_query_pre, w_query, preferred_element_type=jnp.float32
        )
        grad_normed = grad_normed + jnp.einsum(
            "te,de->td", grad_key_pre, w_key, preferred_element_type=jnp.float32
        )
        grad_normed = grad_normed + jnp.einsum(
            "te,de->td", grad_value_pre, w_value, preferred_element_type=jnp.float32
        )
        grad_input, unused_gain = rms_backward(state, inverse1, norm1_gain, grad_normed)
        grad_state = grad_next + grad_input
    front_part = reduce_rows(normed_spread, stacked(factors[4]), order_a)
    down_sum = collect_columns(down_part, column_order, width)
    gate_sum = collect_rows(gate_part, order_a, width)
    up_sum = collect_rows(up_part, order_b, width)
    out_sum = collect_rows(out_part, order_b, width)
    front_sum = collect_rows(front_part, order_a, width)
    share = gate_sum.shape[0]
    first = lax.axis_index("str") * share

    def mine(table):
        return lax.dynamic_slice_in_dim(table, first, share, 0)

    gain1, gain2 = (mine(norm1_gain), mine(norm2_gain))
    query_sum = front_sum[:, :width]
    key_sum = front_sum[:, width : width + key_width]
    value_sum = front_sum[:, width + key_width : width + 2 * key_width]
    router_sum = (front_sum[:, width + 2 * key_width :] / gain1[:, None]).T

    def row_dots(weights, sums):
        return jnp.sum(mine(weights).astype(jnp.float32) * sums, axis=1)

    gain1_sum = (
        row_dots(w_query, query_sum) + row_dots(w_key, key_sum) + row_dots(w_value, value_sum)
    ) / gain1
    gain2_sum = (row_dots(w_gate, gate_sum) + row_dots(w_up, up_sum)) / gain2
    return (
        mixed,
        grad_state[None],
        gain1_sum,
        query_sum,
        key_sum,
        value_sum,
        out_sum,
        gain2_sum,
        gate_sum,
        up_sum,
        down_sum,
        router_sum,
    )


def solution(mesh):
    in_specs = (
        P("str", "seq", None),
        P("str", None),
        P("str", "seq"),
        P("str", "seq", None),
        P(),
        P(),
        P(),
        P(),
        P(),
        P(),
        P(),
        P(),
        P(),
        P(),
    )
    out_specs = (
        P("str", "seq", None),
        P("str", "seq", None),
        P("str"),
        P("str", None),
        P("str", None),
        P("str", None),
        P("str", None),
        P("str"),
        P("str", None),
        P("str", None),
        P("str", None),
        P(None, "str"),
    )
    return jax.shard_map(
        per_device, mesh=mesh, in_specs=in_specs, out_specs=out_specs, check_vma=False
    )
```

```python
import functools
import math

import jax
import jax.numpy as jnp
from jax import lax
from jax.experimental import pallas as pl
from jax.experimental.pallas import tpu as pltpu
from jax.sharding import PartitionSpec as P

HD = 64
R = 3
REACH = 3


EPSILON = 1e-05


def rms_forward(values, gain):
    inverse = lax.rsqrt(jnp.mean(values * values, axis=-1, keepdims=True) + EPSILON)
    return (values * inverse * gain, inverse)


def rms_backward(values, inverse, gain, grad_out):
    scaled = grad_out * gain
    grad_gain = jnp.sum(grad_out * values * inverse, axis=0)
    grad_in = inverse * scaled - values * inverse * inverse * inverse * jnp.mean(
        scaled * values, axis=-1, keepdims=True
    )
    return (grad_in, grad_gain)


def rotate(values, cosine_tab, sine_tab):
    heads = values.reshape(-1, 2, HD // 2, values.shape[-1])
    first, second = (heads[:, 0], heads[:, 1])
    return jnp.stack(
        [first * cosine_tab - second * sine_tab, second * cosine_tab + first * sine_tab], 1
    ).reshape(values.shape)


def unrotate(grads, cosine_tab, sine_tab):
    return rotate(grads, cosine_tab, -sine_tab)


def doc_tables(positions, doc_lengths):
    ends = jnp.cumsum(doc_lengths, dtype=jnp.int32)
    after = positions[:, None] >= ends[None, :]
    doc_index = jnp.sum(after.astype(jnp.int32), axis=1, dtype=jnp.int32)
    offset = jnp.sum(jnp.where(after, doc_lengths[None, :], 0), axis=1, dtype=jnp.int32)
    return (doc_index, positions - offset)


def tile_bias(base, tile, low_key, positions, active):
    rows = active.shape[0]
    keys = base + tile * rows + lax.broadcasted_iota(jnp.int32, (rows, positions.shape[1]), 0)
    own = keys == positions
    seen = (keys >= low_key) & (keys <= positions) & ((active > 0) | own)
    return jnp.where(seen, 0.0, -1e30)


def attend_kernel(places, low_ref, act_ref, query_ref, k0, k1, k2, k3, v0, v1, v2, v3,
                  out_ref, log_ref, bias_ref, key_ref, value_ref, top_ref, sum_ref, acc_ref):
    rows = k0.shape[1]
    heads = query_ref.shape[0] // HD
    first_tile = places[1]
    @pl.when(pl.program_id(0) == 0)
    def _():
        positions = places[0] + lax.broadcasted_iota(jnp.int32, (1, rows), 1)
        for tile in range(REACH + 1):
            @pl.when(tile >= first_tile)
            def _(tile=tile):
                bias_ref[tile] = tile_bias(places[0] - REACH * rows, tile, low_ref[...], positions,
                                           act_ref[tile * rows:(tile + 1) * rows, :])
    even = places[2] == 0
    key_ref[3] = k0[...]
    value_ref[3] = v0[...]
    key_ref[2] = jnp.where(even, k3[...], k1[...])
    value_ref[2] = jnp.where(even, v3[...], v1[...])
    key_ref[1] = k2[...]
    value_ref[1] = v2[...]
    key_ref[0] = jnp.where(even, k1[...], k3[...])
    value_ref[0] = jnp.where(even, v1[...], v3[...])
    query = query_ref[...] * jnp.bfloat16(HD ** (-0.5))
    query = jnp.concatenate([query[i * HD:(i + 1) * HD] for i in range(heads)], 1)

    def scores(tile):
        s = lax.dot_general(key_ref[tile], query, (((0,), (0,)), ((), ())), preferred_element_type=jnp.float32)
        bias = bias_ref[tile]
        return s + jnp.concatenate([bias] * heads, 1)

    s = scores(REACH)
    top = jnp.max(s, axis=0, keepdims=True)
    p = jnp.exp(s - top)
    top_ref[...] = top
    sum_ref[...] = jnp.sum(p, axis=0, keepdims=True)
    acc_ref[...] = jnp.dot(value_ref[REACH], p.astype(jnp.bfloat16), preferred_element_type=jnp.float32)

    def body(tile, carry):
        s = scores(tile)
        old = top_ref[...]
        top = jnp.maximum(old, jnp.max(s, axis=0, keepdims=True))
        p = jnp.exp(s - top)
        keep = jnp.exp(old - top)
        top_ref[...] = top
        sum_ref[...] = sum_ref[...] * keep + jnp.sum(p, axis=0, keepdims=True)
        acc_ref[...] = acc_ref[...] * keep + jnp.dot(value_ref[tile], p.astype(jnp.bfloat16), preferred_element_type=jnp.float32)
        return carry
    lax.fori_loop(first_tile, REACH, body, 0)
    total = sum_ref[...]
    out = (acc_ref[...] / total).astype(jnp.bfloat16)
    for i in range(heads):
        out_ref[i * HD:(i + 1) * HD, :] = out[:, i * rows:(i + 1) * rows]
    log_ref[0] = top_ref[...] + jnp.log(total)


def pair_specs(rows, heads):
    keys = pl.BlockSpec((HD, rows), lambda h, places: (h, 0))
    values = pl.BlockSpec((HD, rows), lambda h, places: (heads + h, 0))
    return [keys] * 4 + [values] * 4


def attend(places, low_key, active, query, pairs):
    width, rows = query.shape
    heads = pairs[0].shape[0] // (2 * HD)
    group = width // heads
    wide = group // HD * rows
    whole = lambda h, places: (0, 0)
    return pl.pallas_call(
        attend_kernel,
        out_shape=(jax.ShapeDtypeStruct((width, rows), jnp.bfloat16),
                   jax.ShapeDtypeStruct((heads, 1, wide), jnp.float32)),
        grid_spec=pltpu.PrefetchScalarGridSpec(
            num_scalar_prefetch=1, grid=(heads,),
            in_specs=[pl.BlockSpec((1, rows), whole), pl.BlockSpec((4 * rows, 1), whole),
                      pl.BlockSpec((group, rows), lambda h, places: (h, 0))] + pair_specs(rows, heads),
            out_specs=(pl.BlockSpec((group, rows), lambda h, places: (h, 0)),
                       pl.BlockSpec((1, 1, wide), lambda h, places: (h, 0, 0))),
            scratch_shapes=[pltpu.VMEM((4, rows, rows), jnp.float32),
                            pltpu.VMEM((4, HD, rows), jnp.bfloat16),
                            pltpu.VMEM((4, HD, rows), jnp.bfloat16),
                            pltpu.VMEM((1, wide), jnp.float32),
                            pltpu.VMEM((1, wide), jnp.float32),
                            pltpu.VMEM((HD, wide), jnp.float32)]),
        cost_estimate=pl.CostEstimate(flops=4 * width * rows * rows * 16, bytes_accessed=4 * width * rows * 2, transcendentals=0),
        name="attend",
    )(places, low_key, active, query, *pairs, *pairs)


def attend_back_kernel(places, low_ref, act_ref, query_ref, out_ref, grad_ref, log_ref, k0, k1, k2, k3, v0, v1, v2, v3,
                       dq_ref, own_ref, prev_ref, bias_ref, key_ref, value_ref, acc_ref):
    rows = k0.shape[1]
    heads = query_ref.shape[0] // HD
    first_tile = places[1]
    @pl.when(pl.program_id(0) == 0)
    def _():
        positions = places[0] + lax.broadcasted_iota(jnp.int32, (1, rows), 1)
        for tile in range(REACH + 1):
            @pl.when(tile >= first_tile)
            def _(tile=tile):
                bias_ref[tile] = tile_bias(places[0] - REACH * rows, tile, low_ref[...], positions,
                                           act_ref[tile * rows:(tile + 1) * rows, :])
    even = places[2] == 0
    key_ref[3] = k0[...]
    value_ref[3] = v0[...]
    key_ref[2] = jnp.where(even, k3[...], k1[...])
    value_ref[2] = jnp.where(even, v3[...], v1[...])
    key_ref[1] = k2[...]
    value_ref[1] = v2[...]
    key_ref[0] = jnp.where(even, k1[...], k3[...])
    value_ref[0] = jnp.where(even, v1[...], v3[...])
    spread = lambda x: jnp.concatenate([x[i * HD:(i + 1) * HD] for i in range(heads)], 1)
    query = spread(query_ref[...] * jnp.bfloat16(HD ** (-0.5)))
    grad = spread(grad_ref[...])
    delta = jnp.sum(grad.astype(jnp.float32) * spread(out_ref[...]).astype(jnp.float32), axis=0, keepdims=True)
    logs = log_ref[0]
    acc_ref[...] = jnp.zeros_like(acc_ref)

    def step(tile):
        s = lax.dot_general(key_ref[tile], query, (((0,), (0,)), ((), ())), preferred_element_type=jnp.float32)
        bias = bias_ref[tile]
        p = jnp.exp(s + jnp.concatenate([bias] * heads, 1) - logs)
        dp = lax.dot_general(value_ref[tile], grad, (((0,), (0,)), ((), ())), preferred_element_type=jnp.float32)
        ds = (p * (dp - delta)).astype(jnp.bfloat16)
        acc_ref[...] += jnp.dot(key_ref[tile], ds, preferred_element_type=jnp.float32)
        dk = lax.dot_general(query, ds, (((1,), (1,)), ((), ())), preferred_element_type=jnp.float32)
        dv = lax.dot_general(grad, p.astype(jnp.bfloat16), (((1,), (1,)), ((), ())), preferred_element_type=jnp.float32)
        return dk, dv

    dk, dv = step(REACH)
    own_ref[0] = dk
    own_ref[1] = dv
    prev_ref[...] = jnp.zeros_like(prev_ref)

    def body(tile, carry):
        dk, dv = step(tile)
        slot = jnp.where(even, tile, REACH - 1 - tile)
        prev_ref[slot, 0] = dk.astype(jnp.bfloat16)
        prev_ref[slot, 1] = dv.astype(jnp.bfloat16)
        return carry
    lax.fori_loop(first_tile, REACH, body, 0)
    dq = acc_ref[...] * (HD ** (-0.5))
    for i in range(heads):
        dq_ref[i * HD:(i + 1) * HD, :] = dq[:, i * rows:(i + 1) * rows]


def attend_back(places, low_key, active, query, out, grad, logs, pairs):
    width, rows = query.shape
    heads = pairs[0].shape[0] // (2 * HD)
    group = width // heads
    wide = group // HD * rows
    whole = lambda h, places: (0, 0)
    mine = pl.BlockSpec((group, rows), lambda h, places: (h, 0))
    own = pl.BlockSpec((2, HD, rows), lambda h, places: (0, h, 0))
    prev = pl.BlockSpec((REACH, 2, HD, rows), lambda h, places: (0, 0, h, 0))
    return pl.pallas_call(
        attend_back_kernel,
        out_shape=(jax.ShapeDtypeStruct((width, rows), jnp.float32),
                   jax.ShapeDtypeStruct((2, heads * HD, rows), jnp.float32),
                   jax.ShapeDtypeStruct((REACH, 2, heads * HD, rows), jnp.bfloat16)),
        grid_spec=pltpu.PrefetchScalarGridSpec(
            num_scalar_prefetch=1, grid=(heads,),
            in_specs=[pl.BlockSpec((1, rows), whole), pl.BlockSpec((4 * rows, 1), whole),
                      mine, mine, mine, pl.BlockSpec((1, 1, wide), lambda h, places: (h, 0, 0))] + pair_specs(rows, heads),
            out_specs=(mine, own, prev),
            scratch_shapes=[pltpu.VMEM((4, rows, rows), jnp.float32),
                            pltpu.VMEM((4, HD, rows), jnp.bfloat16),
                            pltpu.VMEM((4, HD, rows), jnp.bfloat16),
                            pltpu.VMEM((HD, wide), jnp.float32)]),
        cost_estimate=pl.CostEstimate(flops=10 * width * rows * rows * 16, bytes_accessed=8 * width * rows * 2, transcendentals=0),
        name="attend_back",
    )(places, low_key, active, query, out, grad, logs, *pairs, *pairs)


def front_kernel(level, query_ref, own_ref, two_ref, mixed_ref, cos_ref, sin_ref, router_ref, *refs):
    all_ref, now_ref = refs[-2:]
    width = query_ref.shape[0]
    half = HD // 2
    pair = own_ref[...] + two_ref[...].astype(jnp.float32) + mixed_ref[...].astype(jnp.float32)
    key_width = pair.shape[0] // 2
    cosine, sine = (cos_ref[...], sin_ref[...])
    turned = []
    for values in (query_ref[...], pair[:key_width]):
        for head in range(values.shape[0] // HD):
            first = values[head * HD : head * HD + half]
            second = values[head * HD + half : (head + 1) * HD]
            turned.append(first * cosine + second * sine)
            turned.append(second * cosine - first * sine)
    done = jnp.concatenate(turned + [pair[key_width:]], 0).astype(jnp.bfloat16)
    now_ref[...] = done
    all_ref[: width + 2 * key_width, :] = done
    spare = all_ref.shape[0] - done.shape[0]
    place = lax.broadcasted_iota(jnp.int32, (spare, done.shape[1]), 0)
    all_ref[width + 2 * key_width :, :] = jnp.where(place == level, router_ref[...], 0.0).astype(
        jnp.bfloat16
    )


def front(level, query, own, two, mixed, cosine, sine, router_row, collected):
    width, rows = query.shape
    height = width + own.shape[0]
    tall = -(-(height + R) // 128) * 128
    block = pl.BlockSpec((tall, rows), lambda i: (0, level))
    inputs = [query, own, two, mixed, cosine, sine, router_row]
    specs = [pl.BlockSpec(item.shape, lambda i: (0, 0)) for item in inputs]
    aliases = {}
    if collected is not None:
        inputs.append(collected)
        specs.append(pl.BlockSpec(memory_space=pl.ANY))
        aliases = {len(inputs) - 1: 0}
    return pl.pallas_call(
        functools.partial(front_kernel, level),
        grid=(1,),
        out_shape=(
            jax.ShapeDtypeStruct((tall, R * rows), jnp.bfloat16),
            jax.ShapeDtypeStruct((height, rows), jnp.bfloat16),
        ),
        in_specs=specs,
        out_specs=(block, pl.BlockSpec((height, rows), lambda i: (0, 0))),
        input_output_aliases=aliases,
        name="front",
    )(*inputs)


def swap(block, mask):
    devices = range(lax.axis_size("seq"))
    return lax.ppermute(block, "seq", [(i, i ^ mask) for i in devices])


def moved(block, targets):
    devices = range(lax.axis_size("seq"))
    return lax.ppermute(
        block, "seq", [(i, t) for i, t in enumerate(targets) if t in devices]
    )


def halo(block):
    devices = range(lax.axis_size("seq"))
    two = moved(block, [i + 2 for i in devices])
    mixed = moved(block, [i + 1 if i % 2 == 0 else i + 3 for i in devices])
    return (mixed, two, swap(two, 1))


def halo_back(mixed, second, across):
    devices = range(lax.axis_size("seq"))
    across = swap(across, 1)
    mixed = moved(mixed, [i - 1 if i % 2 == 1 else i - 3 for i in devices])
    two = moved(added(second, across), [i - 2 for i in devices])
    return (two, mixed)


def stage_lists():
    devices, streams = (lax.axis_size("seq"), lax.axis_size("str"))
    rest = [("seq", 1 << b) for b in range(1, devices.bit_length() - 1)]
    half = len(rest) // 2
    streams_bits = [("str", (2 << b) - 1) for b in range(streams.bit_length() - 1)]
    x_bits, y_bits = (rest[:half], rest[half:])
    return (
        x_bits + y_bits + streams_bits,
        y_bits + x_bits + streams_bits,
        streams_bits[:1] + x_bits + y_bits + streams_bits[1:],
    )


def exchange(block, stage):
    axis, mask = stage
    devices = range(lax.axis_size(axis))
    return lax.ppermute(block, axis, [(i, i ^ mask) for i in devices])


def offsets(index, stages):
    piece, stream = (index * 0, index * 0)
    for place, (axis, mask) in enumerate(reversed(stages)):
        bit = (index >> place) & 1
        if axis == "seq":
            piece = piece ^ (bit * mask)
        else:
            stream = stream ^ (bit * mask)
    return (piece, stream)


def slot_rows(width):
    devices, streams = (lax.axis_size("seq"), lax.axis_size("str"))
    share = width // streams
    slots = -(-share // devices)
    return (share, -(-slots // 8) * 8)


def one_hot(rows, columns):
    return (rows[:, None] == columns[None, :]).astype(jnp.bfloat16)


def row_spread(width, stages):
    devices, streams = (lax.axis_size("seq"), lax.axis_size("str"))
    share, slots = slot_rows(width)
    index = jnp.arange(devices * streams * slots, dtype=jnp.int32)
    piece, stream = offsets(index // slots, [("seq", 1)] + stages)
    inside = (piece ^ lax.axis_index("seq")) * slots + index % slots
    first = (stream ^ lax.axis_index("str")) * share
    target = jnp.where(inside < share, first + inside, -1)
    return one_hot(jnp.arange(width, dtype=jnp.int32), target)


def seq_only(stages):
    return [("seq", 1)] + [stage for stage in stages if stage[0] == "seq"]


def row_gather(width, stages):
    devices = lax.axis_size("seq")
    share, slots = slot_rows(width)
    index = jnp.arange(devices * slots, dtype=jnp.int32)
    piece, unused_stream = offsets(index // slots, seq_only(stages))
    target = (piece ^ lax.axis_index("seq")) * slots + index % slots
    return one_hot(jnp.arange(share, dtype=jnp.int32), target)


def column_spread(width, stages):
    devices = lax.axis_size("seq")
    used = -(-width // devices)
    lanes = -(-used // 128) * 128
    index = jnp.arange(devices * lanes, dtype=jnp.int32)
    piece, unused_stream = offsets(index // lanes, seq_only(stages))
    slot = index % lanes
    target = jnp.where(slot < used, (piece ^ lax.axis_index("seq")) * used + slot, -1)
    return one_hot(jnp.arange(width, dtype=jnp.int32), target)


def stream_order(values, stages):
    streams = lax.axis_size("str")
    size = values.shape[1] // streams
    bits = [stage for stage in stages if stage[0] == "str"]
    parts = []
    for index in range(streams):
        unused_piece, stream = offsets(index, bits)
        first = (lax.axis_index("str") ^ stream) * size
        parts.append(lax.dynamic_slice_in_dim(values, first, size, 1))
    return jnp.concatenate(parts, 1)


def low_dot(left, right):
    return jnp.dot(left, right, preferred_element_type=jnp.float32).astype(jnp.bfloat16)


def outer(left, right):
    return jnp.einsum("tm,tn->mn", left, right, preferred_element_type=jnp.float32)


def outer_t(left, right):
    return jnp.einsum("tm,nt->mn", left, right, preferred_element_type=jnp.float32)


def added(*terms):
    total = terms[0].astype(jnp.float32)
    for term in terms[1:]:
        total = total + term.astype(jnp.float32)
    return total.astype(jnp.bfloat16)


def after(values, *marks):
    held = lax.optimization_barrier((values, marks))
    return held[0]


def axis_of(stage, by_columns):
    return 1 if by_columns and stage[0] == "seq" else 0


def halves(factors, axis):
    left, right, product = factors
    if axis == 0:
        half = left.shape[1] // 2
        return ((left[:, :half], right, product), (left[:, half:], right, product))
    half = right.shape[1] // 2
    return ((left, right[:, :half], product), (left, right[:, half:], product))


def value(factors):
    left, right, product = factors
    return product(left, right)


def halved(view, axis):
    array, row, column, rows, columns = view
    if axis == 0:
        return (
            (array, row, column, rows // 2, columns),
            (array, row + rows // 2, column, rows // 2, columns),
        )
    return (
        (array, row, column, rows, columns // 2),
        (array, row, column + columns // 2, rows, columns // 2),
    )


def whole_of(array):
    return (array, 0, 0, array.shape[0], array.shape[1])


def part_of(view):
    array, row, column, rows, columns = view
    return lax.slice(array, (row, column), (row + rows, column + columns))


def to_send(views, stage, by_columns, mark):
    axis = axis_of(stage, by_columns)
    pairs = [halved(view, axis) for view in views]
    arrays = after(tuple(view[0] for view in views), mark)
    uppers = [(array,) + pair[1][1:] for array, pair in zip(arrays, pairs)]
    return (added(*[part_of(view) for view in uppers]), [pair[0] for pair in pairs])


def widen(part, stage, by_columns=False):
    return jnp.concatenate([part, exchange(part, stage)], 1 if by_columns else 0)


def stacked(values):
    return jnp.concatenate(values, 0)


def per_device(
    hidden,
    lengths,
    depth,
    cotangent,
    norm1_gain,
    w_query,
    w_key,
    w_value,
    w_out,
    norm2_gain,
    w_gate,
    w_up,
    w_down,
    router,
):
    rows, width = hidden.shape[1:]
    key_width = w_key.shape[1]
    seq_index = lax.axis_index("seq")
    local_pos = seq_index * rows + jnp.arange(rows, dtype=jnp.int32)
    doc_lengths = lengths[0]
    unused_doc, place = doc_tables(local_pos, doc_lengths)
    low_key = (local_pos - place)[None, :]
    window = (seq_index - REACH) * rows
    first_tile = jnp.maximum((low_key[0, 0] - window) // rows, 0)
    even = seq_index % 2
    places = jnp.stack([seq_index * rows, first_tile, even]).astype(jnp.int32)
    half = HD // 2
    freqs = jnp.exp(-math.log(10000.0) * 2.0 * jnp.arange(half, dtype=jnp.float32) / HD)
    angles = freqs[:, None] * place.astype(jnp.float32)[None, :]
    cosine_tab = jnp.cos(angles)
    sine_tab = jnp.sin(angles)
    depth_row = depth[0]
    mixed_depth, two_depth, across_depth = halo(depth_row)
    depth_all = jnp.concatenate(
        [
            jnp.where(even == 0, mixed_depth, across_depth),
            two_depth,
            jnp.where(even == 0, across_depth, mixed_depth),
            depth_row,
        ],
        0,
    )
    router_rows = router.astype(jnp.float32)
    order_a, order_b, order_c = stage_lists()
    spread_a = row_spread(width, order_a)
    spread_b = row_spread(width, order_b)
    spread_c = column_spread(width, order_c)
    state = hidden[0].astype(jnp.float32)
    saved = []
    for level in range(R):
        normed, inverse1 = rms_forward(state, norm1_gain)
        normed_low = normed.astype(jnp.bfloat16)
        key_pre = jnp.dot(normed_low, w_key, preferred_element_type=jnp.float32)
        value_low = low_dot(normed_low, w_value)
        key_low = rotate(key_pre.T, cosine_tab, sine_tab).astype(jnp.bfloat16)
        local_pair = jnp.concatenate([key_low, value_low.T], 0)
        pairs = (local_pair, *halo(local_pair))
        query_pre = jnp.dot(normed_low, w_query, preferred_element_type=jnp.float32)
        query_low = rotate(query_pre.T, cosine_tab, sine_tab).astype(jnp.bfloat16)
        activity = (depth_all > level).astype(jnp.int32)[:, None]
        attended, log_total = attend(places, low_key, activity, query_low, pairs)
        attended_low = attended.T
        attn_out = jnp.dot(attended_low, w_out, preferred_element_type=jnp.float32)
        mid_state = state + attn_out
        normed2, inverse2 = rms_forward(mid_state, norm2_gain)
        normed2_low = after(normed2.astype(jnp.bfloat16))
        gate_pre = jnp.dot(normed2_low, w_gate, preferred_element_type=jnp.float32)
        up_pre = jnp.dot(normed2_low, w_up, preferred_element_type=jnp.float32)
        hidden_act = (jax.nn.silu(gate_pre) * up_pre).astype(jnp.bfloat16)
        ffn_out = jnp.dot(hidden_act, w_down, preferred_element_type=jnp.float32)
        gate_prob = jax.nn.sigmoid(
            jnp.dot(state, router_rows[level], precision=lax.Precision.HIGHEST)
        )
        active = (depth_row > level).astype(jnp.float32)
        both = attn_out + ffn_out
        saved.append(
            (
                state,
                inverse1,
                normed_low,
                query_low,
                pairs,
                activity,
                attended,
                log_total,
                attended_low,
                mid_state,
                inverse2,
                normed2_low,
                gate_pre,
                up_pre,
                hidden_act,
                both,
                gate_prob,
                active,
            )
        )
        state = state + (active * gate_prob)[:, None] * both
    mixed = state.astype(jnp.bfloat16)[None]
    grad_state = cotangent[0]
    front_left = low_dot(stacked([item[2] for item in saved]), spread_b)
    out_left = low_dot(stacked([item[8] for item in saved]), spread_b)
    normed2_all = stacked([item[11] for item in saved])
    gate_left = low_dot(normed2_all, spread_a)
    up_left = low_dot(normed2_all, spread_b)
    down_left = stream_order(stacked([item[14] for item in saved]), order_c)
    rights = {kind: [None] * R for kind in ("down", "gate", "up", "out")}
    collected = None
    weights = jnp.concatenate([w_query, w_key, w_value], 1)
    for level in range(R - 1, -1, -1):
        (
            state,
            inverse1,
            normed_low,
            query_low,
            pairs,
            activity,
            attended,
            log_total,
            attended_low,
            mid_state,
            inverse2,
            unused_low,
            gate_pre,
            up_pre,
            hidden_act,
            both,
            gate_prob,
            active,
        ) = saved[level]
        grad_branch = (active * gate_prob)[:, None] * grad_state
        grad_logit = jnp.sum(grad_state * both, axis=-1) * active * gate_prob * (1.0 - gate_prob)
        grad_next = grad_state + grad_logit[:, None] * router_rows[level][None, :]
        grad_ffn = grad_branch.astype(jnp.bfloat16)
        rights["down"][level] = low_dot(grad_ffn, spread_c)
        if level == 0:
            down_low, down_high = halves((down_left, stacked(rights["down"]), outer), 1)
            down_sent = added(value(down_high))
            down_got = swap(down_sent, 1)
            grad_ffn = after(grad_ffn, down_sent)
        grad_act = jnp.einsum("td,fd->tf", grad_ffn, w_down, preferred_element_type=jnp.float32)
        sigma = jax.nn.sigmoid(gate_pre)
        grad_gate = (grad_act * up_pre * sigma * (1.0 + gate_pre * (1.0 - sigma))).astype(
            jnp.bfloat16
        )
        grad_up_pre = (grad_act * gate_pre * sigma).astype(jnp.bfloat16)
        rights["gate"][level] = grad_gate
        rights["up"][level] = grad_up_pre
        if level == 0:
            gate_low, gate_high = halves((gate_left, stacked(rights["gate"]), outer), 0)
            gate_sent = added(value(gate_high))
            gate_got = swap(gate_sent, 1)
            up_right = after(stacked(rights["up"]), gate_sent)
            up_low, up_high = halves((up_left, up_right, outer), 0)
            up_sent = added(value(up_high))
            up_got = swap(up_sent, 1)
            grad_gate, grad_up_pre = after((grad_gate, grad_up_pre), up_sent)
        grad_normed2 = jnp.einsum(
            "tf,df->td", grad_gate, w_gate, preferred_element_type=jnp.float32
        )
        grad_normed2 = grad_normed2 + jnp.einsum(
            "tf,df->td", grad_up_pre, w_up, preferred_element_type=jnp.float32
        )
        grad_mid, unused_gain = rms_backward(mid_state, inverse2, norm2_gain, grad_normed2)
        grad_next = grad_next + grad_mid
        grad_attn = (grad_branch + grad_mid).astype(jnp.bfloat16)
        spare = -width % 128
        rights["out"][level] = jnp.pad(grad_attn, ((0, 0), (0, spare)))
        if level == 0:
            out_low, out_high = halves((out_left, stacked(rights["out"]), outer), 0)
            out_sent = added(value(out_high))
            out_got = swap(out_sent, 1)

            def second(factors, got, stage, by_columns, mark):
                axis = axis_of(stage, by_columns)
                low, high = halves(factors, axis)
                got_low, got_high = halved(whole_of(got), axis)
                left, right = after(high[:2], mark)
                send = added(outer(left, right), part_of(got_high))
                return (send, low, got_low)

            gate_send, gate_low, gate_kept = second(gate_low, gate_got, order_a[0], False, out_sent)
            down_send, down_low, down_kept = second(
                down_low, down_got, order_c[0], True, gate_send
            )
            up_send, up_low, up_kept = second(up_low, up_got, order_b[0], False, down_send)
            out_send, out_low, out_kept = second(out_low, out_got, order_b[0], False, down_send)
            mix_send = jnp.concatenate([up_send, out_send], 1)
            gate_send, down_send, mix_send = after((gate_send, down_send, mix_send))
            gate_next = exchange(gate_send, order_a[0])
            down_next = exchange(down_send, order_c[0])
            mix_next = exchange(mix_send, order_b[0])
            grad_attn = after(grad_attn, gate_send, down_send, mix_send)
        grad_attended = jnp.einsum(
            "te,de->td", grad_attn, w_out, preferred_element_type=jnp.float32
        ).astype(jnp.bfloat16)
        grad_query, own_pair, prior = attend_back(
            places, low_key, activity, query_low, attended, grad_attended.T, log_total, pairs
        )
        prior = prior.reshape(REACH, -1, rows)
        two, mixed_pair = halo_back(prior[0], prior[1], prior[2])
        if level == 0:

            def kept(factors, view, mark):
                left, right = after(factors[:2], mark)
                return added(outer(left, right), part_of(view))

            gate_base = kept(gate_low, gate_kept, prior)
            down_base = kept(down_low, down_kept, prior)
            mix_base = jnp.concatenate(
                [kept(up_low, up_kept, prior), kept(out_low, out_kept, prior)], 1
            )
            plan = {
                "gate": (order_a, False),
                "down": (order_c, True),
                "mix": (order_b, False),
                "front": (order_b, False),
            }
            views = {
                "gate": [whole_of(gate_base), whole_of(gate_next)],
                "down": [whole_of(down_base), whole_of(down_next)],
                "mix": [whole_of(mix_base), whole_of(mix_next)],
            }
            places_done = {"gate": 1, "down": 1, "mix": 1, "front": 0}

            def step(kind, mark):
                order, by_columns = plan[kind]
                stage = order[places_done[kind]]
                send, lows = to_send(views[kind], stage, by_columns, mark)
                views[kind] = lows + [whole_of(exchange(send, stage))]
                places_done[kind] += 1
                return send

            mark = (prior,)
            for kind in ("gate", "down", "mix"):
                mark = step(kind, mark)
            grad_query = after(grad_query, mark)
        collected, now = front(
            level,
            grad_query,
            own_pair.reshape(-1, rows),
            two,
            mixed_pair,
            cosine_tab,
            sine_tab,
            (grad_logit / inverse1[:, 0])[None, :],
            collected,
        )
        if level == 0:
            front_low, front_high = halves((front_left, collected, outer_t), 0)
            front_sent = added(value(front_high))
            now = after(now, front_sent)
            front_got = swap(front_sent, 1)
        grad_normed = jnp.einsum("et,de->td", now, weights, preferred_element_type=jnp.float32)
        grad_input, unused_gain = rms_backward(state, inverse1, norm1_gain, grad_normed)
        grad_state = grad_next + grad_input
    front_base = added(value(front_low), front_got)
    views["front"] = [whole_of(front_base)]
    last = len(order_a)
    mark = front_base
    kinds = ("front", "gate", "down", "mix")
    while any(places_done[kind] < last for kind in kinds):
        for kind in kinds:
            if places_done[kind] < last:
                mark = step(kind, mark)
    parts = {kind: added(*[part_of(view) for view in views[kind]]) for kind in kinds}
    seq_stages = {
        kind: [stage for stage in reversed(plan[kind][0]) if stage[0] == "seq"] + [("seq", 1)]
        for kind in kinds
    }
    for place in range(len(seq_stages["gate"])):
        parts = {
            kind: widen(part, seq_stages[kind][place], kind == "down")
            for kind, part in parts.items()
        }
    mix_part = parts["mix"]

    def finish(part, order):
        return jnp.dot(row_gather(width, order), part, preferred_element_type=jnp.float32)

    gate_sum = finish(parts["gate"], order_a)
    up_sum = finish(mix_part[:, : w_up.shape[1]], order_b)
    out_sum = finish(mix_part[:, w_up.shape[1] : w_up.shape[1] + width], order_b)
    front_sum = finish(parts["front"], order_b)
    down_sum = jnp.einsum(
        "fm,dm->fd", parts["down"], spread_c, preferred_element_type=jnp.float32
    )
    share = gate_sum.shape[0]
    first = lax.axis_index("str") * share

    def mine(table):
        return lax.dynamic_slice_in_dim(table, first, share, 0)

    gain1, gain2 = (mine(norm1_gain), mine(norm2_gain))
    query_sum = front_sum[:, :width]
    key_sum = front_sum[:, width : width + key_width]
    value_sum = front_sum[:, width + key_width : width + 2 * key_width]
    first_router = width + 2 * key_width
    router_sum = (front_sum[:, first_router : first_router + R] / gain1[:, None]).T

    def row_dots(weights, sums):
        return jnp.sum(mine(weights).astype(jnp.float32) * sums, axis=1)

    gain1_sum = (
        row_dots(w_query, query_sum) + row_dots(w_key, key_sum) + row_dots(w_value, value_sum)
    ) / gain1
    gain2_sum = (row_dots(w_gate, gate_sum) + row_dots(w_up, up_sum)) / gain2
    return (
        mixed,
        grad_state[None],
        gain1_sum,
        query_sum,
        key_sum,
        value_sum,
        out_sum,
        gain2_sum,
        gate_sum,
        up_sum,
        down_sum,
        router_sum,
    )


def solution(mesh):
    in_specs = (
        P("str", "seq", None),
        P("str", None),
        P("str", "seq"),
        P("str", "seq", None),
        P(),
        P(),
        P(),
        P(),
        P(),
        P(),
        P(),
        P(),
        P(),
        P(),
    )
    out_specs = (
        P("str", "seq", None),
        P("str", "seq", None),
        P("str"),
        P("str", None),
        P("str", None),
        P("str", None),
        P("str", None),
        P("str"),
        P("str", None),
        P("str", None),
        P("str", None),
        P(None, "str"),
    )
    return jax.shard_map(
        per_device, mesh=mesh, in_specs=in_specs, out_specs=out_specs, check_vma=False
    )
```

```python
import functools
import math

import jax
import jax.numpy as jnp
from jax import lax
from jax.experimental import pallas as pl
from jax.experimental.pallas import tpu as pltpu
from jax.sharding import PartitionSpec as P

HD = 64
R = 3
REACH = 3


EPSILON = 1e-05


def rms_forward(values, gain):
    inverse = lax.rsqrt(jnp.mean(values * values, axis=-1, keepdims=True) + EPSILON)
    return (values * inverse * gain, inverse)


def rms_backward(values, inverse, gain, grad_out):
    scaled = grad_out * gain
    grad_gain = jnp.sum(grad_out * values * inverse, axis=0)
    grad_in = inverse * scaled - values * inverse * inverse * inverse * jnp.mean(
        scaled * values, axis=-1, keepdims=True
    )
    return (grad_in, grad_gain)


def rotate(values, cosine_tab, sine_tab):
    heads = values.reshape(-1, 2, HD // 2, values.shape[-1])
    first, second = (heads[:, 0], heads[:, 1])
    return jnp.stack(
        [first * cosine_tab - second * sine_tab, second * cosine_tab + first * sine_tab], 1
    ).reshape(values.shape)


def unrotate(grads, cosine_tab, sine_tab):
    return rotate(grads, cosine_tab, -sine_tab)


def doc_tables(positions, doc_lengths):
    ends = jnp.cumsum(doc_lengths, dtype=jnp.int32)
    after = positions[:, None] >= ends[None, :]
    doc_index = jnp.sum(after.astype(jnp.int32), axis=1, dtype=jnp.int32)
    offset = jnp.sum(jnp.where(after, doc_lengths[None, :], 0), axis=1, dtype=jnp.int32)
    return (doc_index, positions - offset)


def tile_bias(base, tile, low_key, positions, active):
    rows = active.shape[0]
    keys = base + tile * rows + lax.broadcasted_iota(jnp.int32, (rows, positions.shape[1]), 0)
    own = keys == positions
    seen = (keys >= low_key) & (keys <= positions) & ((active > 0) | own)
    return jnp.where(seen, 0.0, -1e30)


def gather_tiles(places, tiles, joined_ref):
    own, mixed, two, across = tiles
    rows = own.shape[1]
    even = places[2] == 0
    joined_ref[:, 3 * rows :] = own[...]
    joined_ref[:, 2 * rows : 3 * rows] = jnp.where(even, across[...], mixed[...])
    joined_ref[:, rows : 2 * rows] = two[...]
    joined_ref[:, :rows] = jnp.where(even, mixed[...], across[...])


def fill_bias(places, low_ref, act_ref, bias_ref):
    rows = bias_ref.shape[1]
    @pl.when(pl.program_id(0) == 0)
    def _():
        positions = places[0] + lax.broadcasted_iota(jnp.int32, (1, rows), 1)
        for tile in range(REACH + 1):
            part = slice(tile * rows, (tile + 1) * rows)
            bias_ref[part, :] = tile_bias(places[0] - REACH * rows, tile, low_ref[...], positions,
                                          act_ref[part, :])


def attend_kernel(places, low_ref, act_ref, query_ref, k0, k1, k2, k3, v0, v1, v2, v3,
                  out_ref, log_ref, bias_ref, key_ref, value_ref):
    rows = k0.shape[1]
    heads = query_ref.shape[0] // HD
    fill_bias(places, low_ref, act_ref, bias_ref)
    gather_tiles(places, (k0, k1, k2, k3), key_ref)
    gather_tiles(places, (v0, v1, v2, v3), value_ref)
    keys, values = (key_ref[...].T, value_ref[...])
    for i in range(heads):
        query = query_ref[i * HD:(i + 1) * HD, :] * jnp.bfloat16(HD ** (-0.5))
        s = jnp.dot(keys, query, preferred_element_type=jnp.float32) + bias_ref[...]
        top = jnp.max(s, axis=0, keepdims=True)
        p = jnp.exp(s - top)
        total = jnp.sum(p, axis=0, keepdims=True)
        acc = jnp.dot(values, p.astype(jnp.bfloat16), preferred_element_type=jnp.float32)
        out_ref[i * HD:(i + 1) * HD, :] = (acc / total).astype(jnp.bfloat16)
        log_ref[0, :, i * rows:(i + 1) * rows] = top + jnp.log(total)


def pair_specs(rows, heads):
    keys = pl.BlockSpec((HD, rows), lambda h, places: (h, 0))
    values = pl.BlockSpec((HD, rows), lambda h, places: (heads + h, 0))
    return [keys] * 4 + [values] * 4


def attend(places, low_key, active, query, pairs):
    width, rows = query.shape
    heads = pairs[0].shape[0] // (2 * HD)
    group = width // heads
    wide = group // HD * rows
    whole = lambda h, places: (0, 0)
    return pl.pallas_call(
        attend_kernel,
        out_shape=(jax.ShapeDtypeStruct((width, rows), jnp.bfloat16),
                   jax.ShapeDtypeStruct((heads, 1, wide), jnp.float32)),
        grid_spec=pltpu.PrefetchScalarGridSpec(
            num_scalar_prefetch=1, grid=(heads,),
            in_specs=[pl.BlockSpec((1, rows), whole), pl.BlockSpec((4 * rows, 1), whole),
                      pl.BlockSpec((group, rows), lambda h, places: (h, 0))] + pair_specs(rows, heads),
            out_specs=(pl.BlockSpec((group, rows), lambda h, places: (h, 0)),
                       pl.BlockSpec((1, 1, wide), lambda h, places: (h, 0, 0))),
            scratch_shapes=[pltpu.VMEM(((REACH + 1) * rows, rows), jnp.float32),
                            pltpu.VMEM((HD, (REACH + 1) * rows), jnp.bfloat16),
                            pltpu.VMEM((HD, (REACH + 1) * rows), jnp.bfloat16)]),
        cost_estimate=pl.CostEstimate(flops=4 * width * rows * rows * 16, bytes_accessed=4 * width * rows * 2, transcendentals=0),
        name="attend",
    )(places, low_key, active, query, *pairs, *pairs)


def attend_back_kernel(places, low_ref, act_ref, query_ref, out_ref, grad_ref, log_ref, k0, k1, k2, k3, v0, v1, v2, v3,
                       dq_ref, own_ref, prev_ref, bias_ref, key_ref, value_ref):
    rows = k0.shape[1]
    heads = query_ref.shape[0] // HD
    fill_bias(places, low_ref, act_ref, bias_ref)
    gather_tiles(places, (k0, k1, k2, k3), key_ref)
    gather_tiles(places, (v0, v1, v2, v3), value_ref)
    keys = key_ref[...]
    key_rows, value_rows = (keys.T, value_ref[...].T)
    grad_keys = grad_values = None
    for i in range(heads):
        head = slice(i * HD, (i + 1) * HD)
        query = query_ref[head, :] * jnp.bfloat16(HD ** (-0.5))
        grad = grad_ref[head, :]
        delta = jnp.sum(grad.astype(jnp.float32) * out_ref[head, :].astype(jnp.float32), axis=0, keepdims=True)
        logs = log_ref[0, :, i * rows:(i + 1) * rows]
        p = jnp.exp(jnp.dot(key_rows, query, preferred_element_type=jnp.float32) + bias_ref[...] - logs)
        dp = jnp.dot(value_rows, grad, preferred_element_type=jnp.float32)
        ds = (p * (dp - delta)).astype(jnp.bfloat16)
        dq_ref[head, :] = jnp.dot(keys, ds, preferred_element_type=jnp.float32) * (HD ** (-0.5))
        dk = lax.dot_general(query, ds, (((1,), (1,)), ((), ())), preferred_element_type=jnp.float32)
        dv = lax.dot_general(grad, p.astype(jnp.bfloat16), (((1,), (1,)), ((), ())), preferred_element_type=jnp.float32)
        grad_keys = dk if i == 0 else grad_keys + dk
        grad_values = dv if i == 0 else grad_values + dv
    even = places[2] == 0
    own_ref[0] = grad_keys[:, REACH * rows:]
    own_ref[1] = grad_values[:, REACH * rows:]
    for tile in range(REACH):
        slot = jnp.where(even, tile, REACH - 1 - tile)
        part = slice(tile * rows, (tile + 1) * rows)
        prev_ref[slot, 0] = grad_keys[:, part].astype(jnp.bfloat16)
        prev_ref[slot, 1] = grad_values[:, part].astype(jnp.bfloat16)


def attend_back(places, low_key, active, query, out, grad, logs, pairs):
    width, rows = query.shape
    heads = pairs[0].shape[0] // (2 * HD)
    group = width // heads
    wide = group // HD * rows
    whole = lambda h, places: (0, 0)
    mine = pl.BlockSpec((group, rows), lambda h, places: (h, 0))
    own = pl.BlockSpec((2, HD, rows), lambda h, places: (0, h, 0))
    prev = pl.BlockSpec((REACH, 2, HD, rows), lambda h, places: (0, 0, h, 0))
    return pl.pallas_call(
        attend_back_kernel,
        out_shape=(jax.ShapeDtypeStruct((width, rows), jnp.float32),
                   jax.ShapeDtypeStruct((2, heads * HD, rows), jnp.float32),
                   jax.ShapeDtypeStruct((REACH, 2, heads * HD, rows), jnp.bfloat16)),
        grid_spec=pltpu.PrefetchScalarGridSpec(
            num_scalar_prefetch=1, grid=(heads,),
            in_specs=[pl.BlockSpec((1, rows), whole), pl.BlockSpec((4 * rows, 1), whole),
                      mine, mine, mine, pl.BlockSpec((1, 1, wide), lambda h, places: (h, 0, 0))] + pair_specs(rows, heads),
            out_specs=(mine, own, prev),
            scratch_shapes=[pltpu.VMEM(((REACH + 1) * rows, rows), jnp.float32),
                            pltpu.VMEM((HD, (REACH + 1) * rows), jnp.bfloat16),
                            pltpu.VMEM((HD, (REACH + 1) * rows), jnp.bfloat16)]),
        cost_estimate=pl.CostEstimate(flops=10 * width * rows * rows * 16, bytes_accessed=8 * width * rows * 2, transcendentals=0),
        name="attend_back",
    )(places, low_key, active, query, out, grad, logs, *pairs, *pairs)


def front_kernel(level, query_ref, own_ref, two_ref, mixed_ref, cos_ref, sin_ref, router_ref, *refs):
    all_ref, now_ref = refs[-2:]
    width = query_ref.shape[0]
    half = HD // 2
    pair = own_ref[...] + two_ref[...].astype(jnp.float32) + mixed_ref[...].astype(jnp.float32)
    key_width = pair.shape[0] // 2
    cosine, sine = (cos_ref[...], sin_ref[...])
    turned = []
    for values in (query_ref[...], pair[:key_width]):
        for head in range(values.shape[0] // HD):
            first = values[head * HD : head * HD + half]
            second = values[head * HD + half : (head + 1) * HD]
            turned.append(first * cosine + second * sine)
            turned.append(second * cosine - first * sine)
    rows = pair.shape[1]
    blank = lambda size: jnp.zeros((-size % 128, rows), jnp.float32)
    place = lax.broadcasted_iota(jnp.int32, (-key_width % 128, rows), 0)
    cut = 2 * (width // HD)
    done = jnp.concatenate(
        turned[:cut]
        + [blank(width)]
        + turned[cut:]
        + [blank(key_width), pair[key_width:], jnp.where(place == level, router_ref[...], 0.0)],
        0,
    ).astype(jnp.bfloat16)
    now_ref[...] = done
    all_ref[...] = done


def front(level, query, own, two, mixed, cosine, sine, router_row, collected):
    width, rows = query.shape
    key_width = own.shape[0] // 2
    tall = width + -width % 128 + 2 * (key_width + -key_width % 128)
    block = pl.BlockSpec((tall, rows), lambda i: (0, level))
    inputs = [query, own, two, mixed, cosine, sine, router_row]
    specs = [pl.BlockSpec(item.shape, lambda i: (0, 0)) for item in inputs]
    aliases = {}
    if collected is not None:
        inputs.append(collected)
        specs.append(pl.BlockSpec(memory_space=pl.ANY))
        aliases = {len(inputs) - 1: 0}
    return pl.pallas_call(
        functools.partial(front_kernel, level),
        grid=(1,),
        out_shape=(
            jax.ShapeDtypeStruct((tall, R * rows), jnp.bfloat16),
            jax.ShapeDtypeStruct((tall, rows), jnp.bfloat16),
        ),
        in_specs=specs,
        out_specs=(block, pl.BlockSpec((tall, rows), lambda i: (0, 0))),
        input_output_aliases=aliases,
        name="front",
    )(*inputs)


def swap(block, mask):
    devices = range(lax.axis_size("seq"))
    return lax.ppermute(block, "seq", [(i, i ^ mask) for i in devices])


def moved(block, targets):
    devices = range(lax.axis_size("seq"))
    return lax.ppermute(
        block, "seq", [(i, t) for i, t in enumerate(targets) if t in devices]
    )


def halo(block):
    devices = range(lax.axis_size("seq"))
    two = moved(block, [i + 2 for i in devices])
    mixed = moved(block, [i + 1 if i % 2 == 0 else i + 3 for i in devices])
    return (mixed, two, swap(two, 1))


def halo_back(mixed, second, across):
    devices = range(lax.axis_size("seq"))
    across = swap(across, 1)
    mixed = moved(mixed, [i - 1 if i % 2 == 1 else i - 3 for i in devices])
    second = added(second, across)
    two = moved(second, [i - 2 for i in devices])
    return (two, mixed, second)


def stage_lists():
    devices, streams = (lax.axis_size("seq"), lax.axis_size("str"))
    rest = [("seq", 1 << b) for b in range(1, devices.bit_length() - 1)]
    half = len(rest) // 2
    streams_bits = [("str", (2 << b) - 1) for b in range(streams.bit_length() - 1)]
    x_bits, y_bits = (rest[:half], rest[half:])
    return (
        x_bits + y_bits + streams_bits,
        y_bits + x_bits + streams_bits,
        streams_bits[:1] + y_bits + x_bits + streams_bits[1:],
    )


def exchange(block, stage):
    axis, mask = stage
    devices = range(lax.axis_size(axis))
    return lax.ppermute(block, axis, [(i, i ^ mask) for i in devices])


def offsets(index, stages):
    piece, stream = (index * 0, index * 0)
    for place, (axis, mask) in enumerate(reversed(stages)):
        bit = (index >> place) & 1
        if axis == "seq":
            piece = piece ^ (bit * mask)
        else:
            stream = stream ^ (bit * mask)
    return (piece, stream)


def slot_rows(width):
    devices, streams = (lax.axis_size("seq"), lax.axis_size("str"))
    share = width // streams
    slots = -(-share // devices)
    return (share, -(-slots // 8) * 8)


def one_hot(rows, columns):
    return (rows[:, None] == columns[None, :]).astype(jnp.bfloat16)


def row_spread(width, stages):
    devices, streams = (lax.axis_size("seq"), lax.axis_size("str"))
    share, slots = slot_rows(width)
    index = jnp.arange(devices * streams * slots, dtype=jnp.int32)
    piece, stream = offsets(index // slots, [("seq", 1)] + stages)
    inside = (piece ^ lax.axis_index("seq")) * slots + index % slots
    first = (stream ^ lax.axis_index("str")) * share
    target = jnp.where(inside < share, first + inside, -1)
    return one_hot(jnp.arange(width, dtype=jnp.int32), target)


def seq_only(stages):
    return [("seq", 1)] + [stage for stage in stages if stage[0] == "seq"]


def row_gather(width, stages):
    devices = lax.axis_size("seq")
    share, slots = slot_rows(width)
    index = jnp.arange(devices * slots, dtype=jnp.int32)
    piece, unused_stream = offsets(index // slots, seq_only(stages))
    target = (piece ^ lax.axis_index("seq")) * slots + index % slots
    return one_hot(jnp.arange(share, dtype=jnp.int32), target)


def column_spread(width, stages):
    devices = lax.axis_size("seq")
    used = -(-width // devices)
    lanes = -(-used // 128) * 128
    index = jnp.arange(devices * lanes, dtype=jnp.int32)
    piece, unused_stream = offsets(index // lanes, seq_only(stages))
    slot = index % lanes
    target = jnp.where(slot < used, (piece ^ lax.axis_index("seq")) * used + slot, -1)
    return one_hot(jnp.arange(width, dtype=jnp.int32), target)


def stream_order(values, stages):
    streams = lax.axis_size("str")
    size = values.shape[1] // streams
    bits = [stage for stage in stages if stage[0] == "str"]
    parts = []
    for index in range(streams):
        unused_piece, stream = offsets(index, bits)
        first = (lax.axis_index("str") ^ stream) * size
        parts.append(lax.dynamic_slice_in_dim(values, first, size, 1))
    return jnp.concatenate(parts, 1)


def low_dot(left, right):
    return jnp.dot(left, right, preferred_element_type=jnp.float32).astype(jnp.bfloat16)


def outer(left, right):
    return jnp.einsum("tm,tn->mn", left, right, preferred_element_type=jnp.float32)


def outer_t(left, right):
    return jnp.einsum("tm,nt->mn", left, right, preferred_element_type=jnp.float32)


def added(*terms):
    total = terms[0].astype(jnp.float32)
    for term in terms[1:]:
        total = total + term.astype(jnp.float32)
    return total.astype(jnp.bfloat16)


def after(values, *marks):
    held = lax.optimization_barrier((values, marks))
    return held[0]


def axis_of(stage, by_columns):
    return 1 if by_columns and stage[0] == "seq" else 0


def halves(factors, axis):
    left, right, product = factors
    if axis == 0:
        half = left.shape[1] // 2
        return ((left[:, :half], right, product), (left[:, half:], right, product))
    half = right.shape[1] // 2
    return ((left, right[:, :half], product), (left, right[:, half:], product))


def value(factors):
    left, right, product = factors
    return product(left, right)


def share_of(view, axis, place, parts):
    array, row, column, rows, columns = view
    if axis == 0:
        rows = rows // parts
        return (array, row + place * rows, column, rows, columns)
    columns = columns // parts
    return (array, row, column + place * columns, rows, columns)


def grouped(stages):
    groups = []
    for stage in stages:
        if stage[0] == "str" and groups and groups[-1][0][0] == "str" and len(groups[-1]) < 2:
            groups[-1].append(stage)
        else:
            groups.append([stage])
    return groups


def mask_of(group, place):
    mask = 0
    for bit, stage in enumerate(reversed(group)):
        if (place >> bit) & 1:
            mask ^= stage[1]
    return (group[0][0], mask)


def whole_of(array):
    return (array, 0, 0, array.shape[0], array.shape[1])


def part_of(view):
    array, row, column, rows, columns = view
    return lax.slice(array, (row, column), (row + rows, column + columns))


def to_send(views, group, by_columns, mark):
    axis = axis_of(group[0], by_columns)
    parts = 1 << len(group)
    arrays = after(tuple(view[0] for view in views), mark)
    held = [(array,) + view[1:] for array, view in zip(arrays, views)]
    sends = [
        added(*[part_of(share_of(view, axis, place, parts)) for view in held])
        for place in range(1, parts)
    ]
    return (sends, [share_of(view, axis, 0, parts) for view in views])


def widen_all(part, group, by_columns=False):
    pieces = [part] + [exchange(part, mask_of(group, i)) for i in range(1, 1 << len(group))]
    return jnp.concatenate(pieces, 1 if by_columns else 0)


def stacked(values):
    return jnp.concatenate(values, 0)


def per_device(
    hidden,
    lengths,
    depth,
    cotangent,
    norm1_gain,
    w_query,
    w_key,
    w_value,
    w_out,
    norm2_gain,
    w_gate,
    w_up,
    w_down,
    router,
):
    rows, width = hidden.shape[1:]
    key_width = w_key.shape[1]
    seq_index = lax.axis_index("seq")
    local_pos = seq_index * rows + jnp.arange(rows, dtype=jnp.int32)
    doc_lengths = lengths[0]
    unused_doc, place = doc_tables(local_pos, doc_lengths)
    low_key = (local_pos - place)[None, :]
    window = (seq_index - REACH) * rows
    first_tile = jnp.maximum((low_key[0, 0] - window) // rows, 0)
    even = seq_index % 2
    places = jnp.stack([seq_index * rows, first_tile, even]).astype(jnp.int32)
    half = HD // 2
    freqs = jnp.exp(-math.log(10000.0) * 2.0 * jnp.arange(half, dtype=jnp.float32) / HD)
    angles = freqs[:, None] * place.astype(jnp.float32)[None, :]
    cosine_tab = jnp.cos(angles)
    sine_tab = jnp.sin(angles)
    depth_row = depth[0]
    mixed_depth, two_depth, across_depth = halo(depth_row)
    depth_all = jnp.concatenate(
        [
            jnp.where(even == 0, mixed_depth, across_depth),
            two_depth,
            jnp.where(even == 0, across_depth, mixed_depth),
            depth_row,
        ],
        0,
    )
    router_rows = router.astype(jnp.float32)
    order_a, order_b, order_c = stage_lists()
    spread_a = row_spread(width, order_a)
    spread_b = row_spread(width, order_b)
    spread_c = column_spread(width, order_c)
    state = hidden[0].astype(jnp.float32)
    saved = []
    for level in range(R):
        normed, inverse1 = rms_forward(state, norm1_gain)
        normed_low = normed.astype(jnp.bfloat16)
        key_pre = jnp.dot(normed_low, w_key, preferred_element_type=jnp.float32)
        value_low = low_dot(normed_low, w_value)
        key_low = rotate(key_pre.T, cosine_tab, sine_tab).astype(jnp.bfloat16)
        local_pair = jnp.concatenate([key_low, value_low.T], 0)
        pairs = (local_pair, *halo(local_pair))
        query_pre = jnp.dot(normed_low, w_query, preferred_element_type=jnp.float32)
        query_low = rotate(query_pre.T, cosine_tab, sine_tab).astype(jnp.bfloat16)
        if level == 1:
            weights = jnp.concatenate(
                [
                    jnp.pad(item, ((0, 0), (0, -item.shape[1] % 128)))
                    for item in after((w_query, w_key, w_value), local_pair)
                ],
                1,
            )
            share = width // lax.axis_size("str")
            weights_mine = lax.dynamic_slice_in_dim(
                weights, lax.axis_index("str") * share, share, 0
            )
            query_low = after(query_low, weights, weights_mine)
        activity = (depth_all > level).astype(jnp.int32)[:, None]
        attended, log_total = attend(places, low_key, activity, query_low, pairs)
        attended_low = attended.T
        attn_out = jnp.dot(attended_low, w_out, preferred_element_type=jnp.float32)
        mid_state = state + attn_out
        normed2, inverse2 = rms_forward(mid_state, norm2_gain)
        normed2_low = after(normed2.astype(jnp.bfloat16))
        gate_pre = low_dot(normed2_low, w_gate)
        up_pre = jnp.dot(normed2_low, w_up, preferred_element_type=jnp.float32)
        hidden_act = (jax.nn.silu(gate_pre.astype(jnp.float32)) * up_pre).astype(jnp.bfloat16)
        up_pre = up_pre.astype(jnp.bfloat16)
        ffn_out = jnp.dot(hidden_act, w_down, preferred_element_type=jnp.float32)
        gate_prob = jax.nn.sigmoid(
            jnp.dot(state, router_rows[level], precision=lax.Precision.HIGHEST)
        )
        active = (depth_row > level).astype(jnp.float32)
        both = attn_out + ffn_out
        saved.append(
            (
                state,
                inverse1,
                normed_low,
                query_low,
                pairs,
                activity,
                attended,
                log_total,
                attended_low,
                mid_state,
                inverse2,
                normed2_low,
                gate_pre,
                up_pre,
                hidden_act,
                both,
                gate_prob,
                active,
            )
        )
        state = state + (active * gate_prob)[:, None] * both
    mixed = state.astype(jnp.bfloat16)[None]
    grad_state = cotangent[0]
    normed2_all = stacked([item[11] for item in saved])
    hidden_all = stacked([item[14] for item in saved])
    rights = {kind: [None] * R for kind in ("down", "gate", "up", "out")}
    collected = None
    for level in range(R - 1, -1, -1):
        (
            state,
            inverse1,
            normed_low,
            query_low,
            pairs,
            activity,
            attended,
            log_total,
            attended_low,
            mid_state,
            inverse2,
            unused_low,
            gate_pre,
            up_pre,
            hidden_act,
            both,
            gate_prob,
            active,
        ) = saved[level]
        grad_branch = (active * gate_prob)[:, None] * grad_state
        grad_logit = jnp.sum(grad_state * both, axis=-1) * active * gate_prob * (1.0 - gate_prob)
        grad_next = grad_state + grad_logit[:, None] * router_rows[level][None, :]
        grad_ffn = grad_branch.astype(jnp.bfloat16)
        rights["down"][level] = low_dot(grad_ffn, spread_c)
        if level == 0:
            down_low, down_high = halves((down_left, stacked(rights["down"]), outer), 1)
            down_sent = added(value(down_high))
            down_got = swap(down_sent, 1)
            grad_ffn = after(grad_ffn, down_sent)
        grad_act = jnp.einsum("td,fd->tf", grad_ffn, w_down, preferred_element_type=jnp.float32)
        gate_pre, up_pre = (gate_pre.astype(jnp.float32), up_pre.astype(jnp.float32))
        sigma = jax.nn.sigmoid(gate_pre)
        grad_gate = (grad_act * up_pre * sigma * (1.0 + gate_pre * (1.0 - sigma))).astype(
            jnp.bfloat16
        )
        grad_up_pre = (grad_act * gate_pre * sigma).astype(jnp.bfloat16)
        rights["gate"][level] = grad_gate
        rights["up"][level] = grad_up_pre
        if level == 0:
            gate_low, gate_high = halves((gate_left, stacked(rights["gate"]), outer), 0)
            gate_sent = added(value(gate_high))
            gate_got = swap(gate_sent, 1)
            up_right = after(stacked(rights["up"]), gate_sent)
            up_low, up_high = halves((up_left, up_right, outer), 0)
            up_sent = added(value(up_high))
            up_got = swap(up_sent, 1)
            grad_gate, grad_up_pre = after((grad_gate, grad_up_pre), up_sent)
        grad_normed2 = jnp.einsum(
            "tf,df->td", grad_gate, w_gate, preferred_element_type=jnp.float32
        )
        grad_normed2 = grad_normed2 + jnp.einsum(
            "tf,df->td", grad_up_pre, w_up, preferred_element_type=jnp.float32
        )
        grad_mid, unused_gain = rms_backward(mid_state, inverse2, norm2_gain, grad_normed2)
        grad_next = grad_next + grad_mid
        grad_attn = (grad_branch + grad_mid).astype(jnp.bfloat16)
        spare = -width % 128
        rights["out"][level] = jnp.pad(grad_attn, ((0, 0), (0, spare)))
        if level == 0:
            out_low, out_high = halves((out_left, stacked(rights["out"]), outer), 0)
            out_sent = added(value(out_high))
            out_got = swap(out_sent, 1)

            def second(factors, got, stage, by_columns, mark):
                axis = axis_of(stage, by_columns)
                low, high = halves(factors, axis)
                got_low, got_high = [share_of(whole_of(got), axis, i, 2) for i in range(2)]
                left, right = after(high[:2], mark)
                send = added(high[2](left, right), part_of(got_high))
                return (send, low, got_low)

            gate_send, gate_low, gate_kept = second(gate_low, gate_got, order_a[0], False, out_sent)
            down_send, down_low, down_kept = second(
                down_low, down_got, order_c[0], True, gate_send
            )
            up_send, up_low, up_kept = second(up_low, up_got, order_b[0], False, down_send)
            out_send, out_low, out_kept = second(out_low, out_got, order_b[0], False, down_send)
            mix_send = jnp.concatenate([up_send, out_send], 1)
            gate_send, down_send, mix_send = after((gate_send, down_send, mix_send))
            gate_next = exchange(gate_send, order_a[0])
            down_next = exchange(down_send, order_c[0])
            mix_next = exchange(mix_send, order_b[0])
            grad_attn = after(grad_attn, gate_send, down_send, mix_send)
        grad_attended = jnp.einsum(
            "te,de->td", grad_attn, w_out, preferred_element_type=jnp.float32
        ).astype(jnp.bfloat16)
        grad_query, own_pair, prior = attend_back(
            places, low_key, activity, query_low, attended, grad_attended.T, log_total, pairs
        )
        prior = prior.reshape(REACH, -1, rows)
        two, mixed_pair, second_sum = halo_back(prior[0], prior[1], prior[2])
        if level == R - 1:
            attended_all, normed_all = after(
                (stacked([item[8] for item in saved]), stacked([item[2] for item in saved])),
                second_sum,
            )
            out_left = low_dot(attended_all, spread_b)
            front_left = low_dot(normed_all, spread_a)
        if level == R - 2:
            normed2_all, hidden_all = after((normed2_all, hidden_all), second_sum)
            gate_left = low_dot(normed2_all, spread_a)
            up_left = low_dot(normed2_all, spread_b)
            down_left = stream_order(hidden_all, order_c)
        if level == 0:

            def kept(factors, view, mark):
                left, right = after(factors[:2], mark)
                return added(factors[2](left, right), part_of(view))

            gate_base = kept(gate_low, gate_kept, prior)
            down_base = kept(down_low, down_kept, prior)
            mix_base = jnp.concatenate(
                [kept(up_low, up_kept, prior), kept(out_low, out_kept, prior)], 1
            )
            plan = {
                "gate": (order_a, False),
                "down": (order_c, True),
                "mix": (order_b, False),
                "front": (order_a, False),
            }
            views = {
                "gate": [whole_of(gate_base), whole_of(gate_next)],
                "down": [whole_of(down_base), whole_of(down_next)],
                "mix": [whole_of(mix_base), whole_of(mix_next)],
            }
            places_done = {"gate": 1, "down": 1, "mix": 1, "front": 0}

            groups = {kind: grouped(plan[kind][0]) for kind in plan}

            def step(kind, mark):
                group, by_columns = (groups[kind][places_done[kind]], plan[kind][1])
                sends, lows = to_send(views[kind], group, by_columns, mark)
                got = [exchange(send, mask_of(group, i + 1)) for i, send in enumerate(sends)]
                views[kind] = lows + [whole_of(block) for block in got]
                places_done[kind] += 1
                return tuple(sends)

            mark = (prior,)
            for kind in ("gate", "down", "mix"):
                mark = step(kind, mark)
            grad_query = after(grad_query, mark)
        collected, now = front(
            level,
            grad_query,
            own_pair.reshape(-1, rows),
            two,
            mixed_pair,
            cosine_tab,
            sine_tab,
            (grad_logit / inverse1[:, 0])[None, :],
            collected,
        )
        if level == 0:
            front_low, front_high = halves((front_left, collected, outer_t), 0)
            front_sent = added(value(front_high))
            front_got = swap(front_sent, 1)
            front_send, front_low, front_kept = second(
                front_low, front_got, order_a[0], False, mark
            )
            front_next = exchange(front_send, order_a[0])
            now = after(now, front_send)
            mark = front_send
            front_base = kept(front_low, front_kept, front_send)
            views["front"] = [whole_of(front_base), whole_of(front_next)]
            places_done["front"] = 1
        grad_normed = jnp.einsum("et,de->td", now, weights, preferred_element_type=jnp.float32)
        grad_input, unused_gain = rms_backward(state, inverse1, norm1_gain, grad_normed)
        grad_state = grad_next + grad_input
    kinds = ("gate", "down", "mix", "front")
    while any(places_done[kind] < len(groups[kind]) for kind in kinds):
        for kind in kinds:
            if places_done[kind] < len(groups[kind]):
                mark = step(kind, mark)
    parts = {kind: added(*[part_of(view) for view in views[kind]]) for kind in kinds}
    for kind in kinds:
        stages = [stage for stage in plan[kind][0] if stage[0] == "seq"]
        while stages:
            parts[kind] = widen_all(parts[kind], stages[-2:], plan[kind][1])
            stages = stages[:-2]
        parts[kind] = widen_all(parts[kind], [("seq", 1)], plan[kind][1])
    mix_part = parts["mix"]

    def finish(part, order):
        return jnp.dot(row_gather(width, order), part, preferred_element_type=jnp.float32)

    gate_sum = finish(parts["gate"], order_a)
    up_sum = finish(mix_part[:, : w_up.shape[1]], order_b)
    out_sum = finish(mix_part[:, w_up.shape[1] : w_up.shape[1] + width], order_b)
    front_sum = finish(parts["front"], order_a)
    down_sum = jnp.einsum(
        "fm,dm->fd", parts["down"], spread_c, preferred_element_type=jnp.float32
    )
    share = gate_sum.shape[0]
    first = lax.axis_index("str") * share

    def mine(table):
        return lax.dynamic_slice_in_dim(table, first, share, 0)

    gain1, gain2 = (mine(norm1_gain), mine(norm2_gain))
    first_key = width + -width % 128
    first_value = first_key + key_width + -key_width % 128
    query_sum = front_sum[:, :width]
    key_sum = front_sum[:, first_key : first_key + key_width]
    value_sum = front_sum[:, first_value : first_value + key_width]
    first_router = first_value + key_width
    router_sum = (front_sum[:, first_router : first_router + R] / gain1[:, None]).T

    def row_dots(weights, sums):
        return jnp.sum(mine(weights).astype(jnp.float32) * sums, axis=1)

    gain1_sum = jnp.sum(weights_mine.astype(jnp.float32) * front_sum, axis=1) / gain1
    gain2_sum = (row_dots(w_gate, gate_sum) + row_dots(w_up, up_sum)) / gain2
    return (
        mixed,
        grad_state[None],
        gain1_sum,
        query_sum,
        key_sum,
        value_sum,
        out_sum,
        gain2_sum,
        gate_sum,
        up_sum,
        down_sum,
        router_sum,
    )


def solution(mesh):
    in_specs = (
        P("str", "seq", None),
        P("str", None),
        P("str", "seq"),
        P("str", "seq", None),
        P(),
        P(),
        P(),
        P(),
        P(),
        P(),
        P(),
        P(),
        P(),
        P(),
    )
    out_specs = (
        P("str", "seq", None),
        P("str", "seq", None),
        P("str"),
        P("str", None),
        P("str", None),
        P("str", None),
        P("str", None),
        P("str"),
        P("str", None),
        P("str", None),
        P("str", None),
        P(None, "str"),
    )
    return jax.shard_map(
        per_device, mesh=mesh, in_specs=in_specs, out_specs=out_specs, check_vma=False
    )
```

```python
import functools
import math

import jax
import jax.numpy as jnp
from jax import lax
from jax.experimental import pallas as pl
from jax.experimental.pallas import tpu as pltpu
from jax.sharding import PartitionSpec as P

HD = 64
R = 3
REACH = 3


EPSILON = 1e-05


def rms_forward(values, gain):
    inverse = lax.rsqrt(jnp.mean(values * values, axis=-1, keepdims=True) + EPSILON)
    return (values * inverse * gain, inverse)


def rms_backward(values, inverse, gain, grad_out):
    scaled = grad_out * gain
    grad_gain = jnp.sum(grad_out * values * inverse, axis=0)
    grad_in = inverse * scaled - values * inverse * inverse * inverse * jnp.mean(
        scaled * values, axis=-1, keepdims=True
    )
    return (grad_in, grad_gain)


def rotate(values, cosine_tab, sine_tab):
    heads = values.reshape(-1, 2, HD // 2, values.shape[-1])
    first, second = (heads[:, 0], heads[:, 1])
    return jnp.stack(
        [first * cosine_tab - second * sine_tab, second * cosine_tab + first * sine_tab], 1
    ).reshape(values.shape)


def unrotate(grads, cosine_tab, sine_tab):
    return rotate(grads, cosine_tab, -sine_tab)


def doc_tables(positions, doc_lengths):
    ends = jnp.cumsum(doc_lengths, dtype=jnp.int32)
    after = positions[:, None] >= ends[None, :]
    doc_index = jnp.sum(after.astype(jnp.int32), axis=1, dtype=jnp.int32)
    offset = jnp.sum(jnp.where(after, doc_lengths[None, :], 0), axis=1, dtype=jnp.int32)
    return (doc_index, positions - offset)


def tile_bias(base, tile, low_key, positions, active):
    rows = active.shape[0]
    keys = base + tile * rows + lax.broadcasted_iota(jnp.int32, (rows, positions.shape[1]), 0)
    own = keys == positions
    seen = (keys >= low_key) & (keys <= positions) & ((active > 0) | own)
    return jnp.where(seen, 0.0, -1e30)


def gather_tiles(places, tiles, joined_ref):
    own, mixed, two, across = tiles
    rows = own.shape[1]
    even = places[2] == 0
    joined_ref[:, 3 * rows :] = own[...]
    joined_ref[:, 2 * rows : 3 * rows] = jnp.where(even, across[...], mixed[...])
    joined_ref[:, rows : 2 * rows] = two[...]
    joined_ref[:, :rows] = jnp.where(even, mixed[...], across[...])


def fill_bias(places, low_ref, act_ref, bias_ref):
    rows = bias_ref.shape[1]
    @pl.when(pl.program_id(0) == 0)
    def _():
        positions = places[0] + lax.broadcasted_iota(jnp.int32, (1, rows), 1)
        for tile in range(REACH + 1):
            part = slice(tile * rows, (tile + 1) * rows)
            bias_ref[part, :] = tile_bias(places[0] - REACH * rows, tile, low_ref[...], positions,
                                          act_ref[part, :])


def attend_kernel(places, low_ref, act_ref, query_ref, k0, k1, k2, k3, v0, v1, v2, v3,
                  out_ref, log_ref, bias_ref, key_ref, value_ref):
    rows = k0.shape[1]
    heads = query_ref.shape[0] // HD
    fill_bias(places, low_ref, act_ref, bias_ref)
    gather_tiles(places, (k0, k1, k2, k3), key_ref)
    gather_tiles(places, (v0, v1, v2, v3), value_ref)
    keys, values = (key_ref[...].T, value_ref[...])
    for i in range(heads):
        query = query_ref[i * HD:(i + 1) * HD, :] * jnp.bfloat16(HD ** (-0.5))
        s = jnp.dot(keys, query, preferred_element_type=jnp.float32) + bias_ref[...]
        top = jnp.max(s, axis=0, keepdims=True)
        p = jnp.exp(s - top)
        total = jnp.sum(p, axis=0, keepdims=True)
        acc = jnp.dot(values, p.astype(jnp.bfloat16), preferred_element_type=jnp.float32)
        out_ref[i * HD:(i + 1) * HD, :] = (acc / total).astype(jnp.bfloat16)
        log_ref[0, :, i * rows:(i + 1) * rows] = top + jnp.log(total)


def pair_specs(rows, heads):
    keys = pl.BlockSpec((HD, rows), lambda h, places: (h, 0))
    values = pl.BlockSpec((HD, rows), lambda h, places: (heads + h, 0))
    return [keys] * 4 + [values] * 4


def attend(places, low_key, active, query, pairs):
    width, rows = query.shape
    heads = pairs[0].shape[0] // (2 * HD)
    group = width // heads
    wide = group // HD * rows
    whole = lambda h, places: (0, 0)
    return pl.pallas_call(
        attend_kernel,
        out_shape=(jax.ShapeDtypeStruct((width, rows), jnp.bfloat16),
                   jax.ShapeDtypeStruct((heads, 1, wide), jnp.float32)),
        grid_spec=pltpu.PrefetchScalarGridSpec(
            num_scalar_prefetch=1, grid=(heads,),
            in_specs=[pl.BlockSpec((1, rows), whole), pl.BlockSpec((4 * rows, 1), whole),
                      pl.BlockSpec((group, rows), lambda h, places: (h, 0))] + pair_specs(rows, heads),
            out_specs=(pl.BlockSpec((group, rows), lambda h, places: (h, 0)),
                       pl.BlockSpec((1, 1, wide), lambda h, places: (h, 0, 0))),
            scratch_shapes=[pltpu.VMEM(((REACH + 1) * rows, rows), jnp.float32),
                            pltpu.VMEM((HD, (REACH + 1) * rows), jnp.bfloat16),
                            pltpu.VMEM((HD, (REACH + 1) * rows), jnp.bfloat16)]),
        cost_estimate=pl.CostEstimate(flops=4 * width * rows * rows * 16, bytes_accessed=4 * width * rows * 2, transcendentals=0),
        compiler_params=pltpu.CompilerParams(vmem_limit_bytes=12 << 20),
        name="attend",
    )(places, low_key, active, query, *pairs, *pairs)


def attend_back_kernel(places, low_ref, act_ref, query_ref, out_ref, grad_ref, log_ref, k0, k1, k2, k3, v0, v1, v2, v3,
                       dq_ref, own_ref, prev_ref, bias_ref, key_ref, value_ref):
    rows = k0.shape[1]
    heads = query_ref.shape[0] // HD
    fill_bias(places, low_ref, act_ref, bias_ref)
    gather_tiles(places, (k0, k1, k2, k3), key_ref)
    gather_tiles(places, (v0, v1, v2, v3), value_ref)
    keys = key_ref[...]
    key_rows, value_rows = (keys.T, value_ref[...].T)
    grad_keys = grad_values = None
    for i in range(heads):
        head = slice(i * HD, (i + 1) * HD)
        query = query_ref[head, :] * jnp.bfloat16(HD ** (-0.5))
        grad = grad_ref[head, :]
        delta = jnp.sum(grad.astype(jnp.float32) * out_ref[head, :].astype(jnp.float32), axis=0, keepdims=True)
        logs = log_ref[0, :, i * rows:(i + 1) * rows]
        p = jnp.exp(jnp.dot(key_rows, query, preferred_element_type=jnp.float32) + bias_ref[...] - logs)
        dp = jnp.dot(value_rows, grad, preferred_element_type=jnp.float32)
        ds = (p * (dp - delta)).astype(jnp.bfloat16)
        dq_ref[head, :] = jnp.dot(keys, ds, preferred_element_type=jnp.float32) * (HD ** (-0.5))
        dk = lax.dot_general(query, ds, (((1,), (1,)), ((), ())), preferred_element_type=jnp.float32)
        dv = lax.dot_general(grad, p.astype(jnp.bfloat16), (((1,), (1,)), ((), ())), preferred_element_type=jnp.float32)
        grad_keys = dk if i == 0 else grad_keys + dk
        grad_values = dv if i == 0 else grad_values + dv
    even = places[2] == 0
    own_ref[0] = grad_keys[:, REACH * rows:]
    own_ref[1] = grad_values[:, REACH * rows:]
    for tile in range(REACH):
        slot = jnp.where(even, tile, REACH - 1 - tile)
        part = slice(tile * rows, (tile + 1) * rows)
        prev_ref[slot, 0] = grad_keys[:, part].astype(jnp.bfloat16)
        prev_ref[slot, 1] = grad_values[:, part].astype(jnp.bfloat16)


def attend_back(places, low_key, active, query, out, grad, logs, pairs):
    width, rows = query.shape
    heads = pairs[0].shape[0] // (2 * HD)
    group = width // heads
    wide = group // HD * rows
    whole = lambda h, places: (0, 0)
    mine = pl.BlockSpec((group, rows), lambda h, places: (h, 0))
    own = pl.BlockSpec((2, HD, rows), lambda h, places: (0, h, 0))
    prev = pl.BlockSpec((REACH, 2, HD, rows), lambda h, places: (0, 0, h, 0))
    return pl.pallas_call(
        attend_back_kernel,
        out_shape=(jax.ShapeDtypeStruct((width, rows), jnp.float32),
                   jax.ShapeDtypeStruct((2, heads * HD, rows), jnp.float32),
                   jax.ShapeDtypeStruct((REACH, 2, heads * HD, rows), jnp.bfloat16)),
        grid_spec=pltpu.PrefetchScalarGridSpec(
            num_scalar_prefetch=1, grid=(heads,),
            in_specs=[pl.BlockSpec((1, rows), whole), pl.BlockSpec((4 * rows, 1), whole),
                      mine, mine, mine, pl.BlockSpec((1, 1, wide), lambda h, places: (h, 0, 0))] + pair_specs(rows, heads),
            out_specs=(mine, own, prev),
            scratch_shapes=[pltpu.VMEM(((REACH + 1) * rows, rows), jnp.float32),
                            pltpu.VMEM((HD, (REACH + 1) * rows), jnp.bfloat16),
                            pltpu.VMEM((HD, (REACH + 1) * rows), jnp.bfloat16)]),
        cost_estimate=pl.CostEstimate(flops=10 * width * rows * rows * 16, bytes_accessed=8 * width * rows * 2, transcendentals=0),
        compiler_params=pltpu.CompilerParams(vmem_limit_bytes=16 << 20),
        name="attend_back",
    )(places, low_key, active, query, out, grad, logs, *pairs, *pairs)


def front_kernel(level, query_ref, own_ref, two_ref, mixed_ref, cos_ref, sin_ref, router_ref, *refs):
    all_ref, now_ref = refs[-2:]
    width = query_ref.shape[0]
    half = HD // 2
    pair = own_ref[...] + two_ref[...].astype(jnp.float32) + mixed_ref[...].astype(jnp.float32)
    key_width = pair.shape[0] // 2
    cosine, sine = (cos_ref[...], sin_ref[...])
    turned = []
    for values in (query_ref[...], pair[:key_width]):
        for head in range(values.shape[0] // HD):
            first = values[head * HD : head * HD + half]
            second = values[head * HD + half : (head + 1) * HD]
            turned.append(first * cosine + second * sine)
            turned.append(second * cosine - first * sine)
    rows = pair.shape[1]
    blank = lambda size: jnp.zeros((-size % 128, rows), jnp.float32)
    place = lax.broadcasted_iota(jnp.int32, (-key_width % 128, rows), 0)
    cut = 2 * (width // HD)
    done = jnp.concatenate(
        turned[:cut]
        + [blank(width)]
        + turned[cut:]
        + [blank(key_width), pair[key_width:], jnp.where(place == level, router_ref[...], 0.0)],
        0,
    ).astype(jnp.bfloat16)
    now_ref[...] = done
    all_ref[...] = done


def front(level, query, own, two, mixed, cosine, sine, router_row, collected):
    width, rows = query.shape
    key_width = own.shape[0] // 2
    tall = width + -width % 128 + 2 * (key_width + -key_width % 128)
    block = pl.BlockSpec((tall, rows), lambda i: (0, level))
    inputs = [query, own, two, mixed, cosine, sine, router_row]
    specs = [pl.BlockSpec(item.shape, lambda i: (0, 0)) for item in inputs]
    aliases = {}
    if collected is not None:
        inputs.append(collected)
        specs.append(pl.BlockSpec(memory_space=pl.ANY))
        aliases = {len(inputs) - 1: 0}
    return pl.pallas_call(
        functools.partial(front_kernel, level),
        grid=(1,),
        out_shape=(
            jax.ShapeDtypeStruct((tall, R * rows), jnp.bfloat16),
            jax.ShapeDtypeStruct((tall, rows), jnp.bfloat16),
        ),
        in_specs=specs,
        out_specs=(block, pl.BlockSpec((tall, rows), lambda i: (0, 0))),
        input_output_aliases=aliases,
        compiler_params=pltpu.CompilerParams(vmem_limit_bytes=12 << 20),
        name="front",
    )(*inputs)


def swap(block, mask):
    devices = range(lax.axis_size("seq"))
    return lax.ppermute(block, "seq", [(i, i ^ mask) for i in devices])


def moved(block, targets):
    devices = range(lax.axis_size("seq"))
    return lax.ppermute(
        block, "seq", [(i, t) for i, t in enumerate(targets) if t in devices]
    )


def halo(block):
    devices = range(lax.axis_size("seq"))
    two = moved(block, [i + 2 for i in devices])
    mixed = moved(block, [i + 1 if i % 2 == 0 else i + 3 for i in devices])
    return (mixed, two, swap(two, 1))


def halo_back(mixed, second, across):
    devices = range(lax.axis_size("seq"))
    across = swap(across, 1)
    mixed = moved(mixed, [i - 1 if i % 2 == 1 else i - 3 for i in devices])
    second = added(second, across)
    two = moved(second, [i - 2 for i in devices])
    return (two, mixed, second)


def stage_lists():
    devices, streams = (lax.axis_size("seq"), lax.axis_size("str"))
    rest = [("seq", 1 << b) for b in range(1, devices.bit_length() - 1)]
    half = len(rest) // 2
    streams_bits = [("str", (2 << b) - 1) for b in range(streams.bit_length() - 1)]
    x_bits, y_bits = (rest[:half], rest[half:])
    return (
        x_bits + y_bits + streams_bits,
        y_bits + x_bits + streams_bits,
        streams_bits[:1] + y_bits + x_bits + streams_bits[1:],
    )


def exchange(block, stage):
    axis, mask = stage
    devices = range(lax.axis_size(axis))
    return lax.ppermute(block, axis, [(i, i ^ mask) for i in devices])


def offsets(index, stages):
    piece, stream = (index * 0, index * 0)
    for place, (axis, mask) in enumerate(reversed(stages)):
        bit = (index >> place) & 1
        if axis == "seq":
            piece = piece ^ (bit * mask)
        else:
            stream = stream ^ (bit * mask)
    return (piece, stream)


def slot_rows(width):
    devices, streams = (lax.axis_size("seq"), lax.axis_size("str"))
    share = width // streams
    slots = -(-share // devices)
    return (share, -(-slots // 8) * 8)


def one_hot(rows, columns):
    return (rows[:, None] == columns[None, :]).astype(jnp.bfloat16)


def row_spread(width, stages):
    devices, streams = (lax.axis_size("seq"), lax.axis_size("str"))
    share, slots = slot_rows(width)
    index = jnp.arange(devices * streams * slots, dtype=jnp.int32)
    piece, stream = offsets(index // slots, [("seq", 1)] + stages)
    inside = (piece ^ lax.axis_index("seq")) * slots + index % slots
    first = (stream ^ lax.axis_index("str")) * share
    target = jnp.where(inside < share, first + inside, -1)
    return one_hot(jnp.arange(width, dtype=jnp.int32), target)


def seq_only(stages):
    return [("seq", 1)] + [stage for stage in stages if stage[0] == "seq"]


def row_gather(width, stages):
    devices = lax.axis_size("seq")
    share, slots = slot_rows(width)
    index = jnp.arange(devices * slots, dtype=jnp.int32)
    piece, unused_stream = offsets(index // slots, seq_only(stages))
    target = (piece ^ lax.axis_index("seq")) * slots + index % slots
    return one_hot(jnp.arange(share, dtype=jnp.int32), target)


def column_spread(width, stages):
    devices = lax.axis_size("seq")
    used = -(-width // devices)
    lanes = -(-used // 128) * 128
    index = jnp.arange(devices * lanes, dtype=jnp.int32)
    piece, unused_stream = offsets(index // lanes, seq_only(stages))
    slot = index % lanes
    target = jnp.where(slot < used, (piece ^ lax.axis_index("seq")) * used + slot, -1)
    return one_hot(jnp.arange(width, dtype=jnp.int32), target)


def stream_order(values, stages):
    streams = lax.axis_size("str")
    size = values.shape[1] // streams
    bits = [stage for stage in stages if stage[0] == "str"]
    parts = []
    for index in range(streams):
        unused_piece, stream = offsets(index, bits)
        first = (lax.axis_index("str") ^ stream) * size
        parts.append(lax.dynamic_slice_in_dim(values, first, size, 1))
    return jnp.concatenate(parts, 1)


def low_dot(left, right):
    return jnp.dot(left, right, preferred_element_type=jnp.float32).astype(jnp.bfloat16)


def outer(left, right):
    return jnp.einsum("tm,tn->mn", left, right, preferred_element_type=jnp.float32)


def outer_t(left, right):
    return jnp.einsum("tm,nt->mn", left, right, preferred_element_type=jnp.float32)


def added(*terms):
    total = terms[0].astype(jnp.float32)
    for term in terms[1:]:
        total = total + term.astype(jnp.float32)
    return total.astype(jnp.bfloat16)


def after(values, *marks):
    held = lax.optimization_barrier((values, marks))
    return held[0]


def axis_of(stage, by_columns):
    return 1 if by_columns and stage[0] == "seq" else 0


def halves(factors, axis):
    left, right, product = factors
    if axis == 0:
        half = left.shape[1] // 2
        return ((left[:, :half], right, product), (left[:, half:], right, product))
    half = right.shape[1] // 2
    return ((left, right[:, :half], product), (left, right[:, half:], product))


def value(factors):
    left, right, product = factors
    return product(left, right)


def share_of(view, axis, place, parts):
    array, row, column, rows, columns = view
    if axis == 0:
        rows = rows // parts
        return (array, row + place * rows, column, rows, columns)
    columns = columns // parts
    return (array, row, column + place * columns, rows, columns)


def grouped(stages):
    groups = []
    for stage in stages:
        if stage[0] == "str" and groups and groups[-1][0][0] == "str" and len(groups[-1]) < 2:
            groups[-1].append(stage)
        else:
            groups.append([stage])
    return groups


def mask_of(group, place):
    mask = 0
    for bit, stage in enumerate(reversed(group)):
        if (place >> bit) & 1:
            mask ^= stage[1]
    return (group[0][0], mask)


def whole_of(array):
    return (array, 0, 0, array.shape[0], array.shape[1])


def part_of(view):
    array, row, column, rows, columns = view
    return lax.slice(array, (row, column), (row + rows, column + columns))


def to_send(views, group, by_columns, mark):
    axis = axis_of(group[0], by_columns)
    parts = 1 << len(group)
    arrays = after(tuple(view[0] for view in views), mark)
    held = [(array,) + view[1:] for array, view in zip(arrays, views)]
    sends = [
        added(*[part_of(share_of(view, axis, place, parts)) for view in held])
        for place in range(1, parts)
    ]
    return (sends, [share_of(view, axis, 0, parts) for view in views])


def widen_all(part, group, by_columns=False):
    pieces = [part] + [exchange(part, mask_of(group, i)) for i in range(1, 1 << len(group))]
    return jnp.concatenate(pieces, 1 if by_columns else 0)


def stacked(values):
    return jnp.concatenate(values, 0)


def per_device(
    hidden,
    lengths,
    depth,
    cotangent,
    norm1_gain,
    w_query,
    w_key,
    w_value,
    w_out,
    norm2_gain,
    w_gate,
    w_up,
    w_down,
    router,
):
    rows, width = hidden.shape[1:]
    key_width = w_key.shape[1]
    seq_index = lax.axis_index("seq")
    local_pos = seq_index * rows + jnp.arange(rows, dtype=jnp.int32)
    doc_lengths = lengths[0]
    unused_doc, place = doc_tables(local_pos, doc_lengths)
    low_key = (local_pos - place)[None, :]
    window = (seq_index - REACH) * rows
    first_tile = jnp.maximum((low_key[0, 0] - window) // rows, 0)
    even = seq_index % 2
    places = jnp.stack([seq_index * rows, first_tile, even]).astype(jnp.int32)
    half = HD // 2
    freqs = jnp.exp(-math.log(10000.0) * 2.0 * jnp.arange(half, dtype=jnp.float32) / HD)
    angles = freqs[:, None] * place.astype(jnp.float32)[None, :]
    cosine_tab = jnp.cos(angles)
    sine_tab = jnp.sin(angles)
    depth_row = depth[0]
    mixed_depth, two_depth, across_depth = halo(depth_row)
    depth_all = jnp.concatenate(
        [
            jnp.where(even == 0, mixed_depth, across_depth),
            two_depth,
            jnp.where(even == 0, across_depth, mixed_depth),
            depth_row,
        ],
        0,
    )
    router_rows = router.astype(jnp.float32)
    order_a, order_b, order_c = stage_lists()
    spread_a = row_spread(width, order_a)
    spread_b = row_spread(width, order_b)
    spread_c = column_spread(width, order_c)
    state = hidden[0].astype(jnp.float32)
    saved = []
    for level in range(R):
        normed, inverse1 = rms_forward(state, norm1_gain)
        normed_low = normed.astype(jnp.bfloat16)
        key_pre = jnp.dot(normed_low, w_key, preferred_element_type=jnp.float32)
        value_low = low_dot(normed_low, w_value)
        key_low = rotate(key_pre.T, cosine_tab, sine_tab).astype(jnp.bfloat16)
        local_pair = jnp.concatenate([key_low, value_low.T], 0)
        pairs = (local_pair, *halo(local_pair))
        query_pre = jnp.dot(normed_low, w_query, preferred_element_type=jnp.float32)
        query_low = rotate(query_pre.T, cosine_tab, sine_tab).astype(jnp.bfloat16)
        if level == 1:
            weights = jnp.concatenate(
                [
                    jnp.pad(item, ((0, 0), (0, -item.shape[1] % 128)))
                    for item in after((w_query, w_key, w_value), local_pair)
                ],
                1,
            )
            share = width // lax.axis_size("str")
            weights_mine = lax.dynamic_slice_in_dim(
                weights, lax.axis_index("str") * share, share, 0
            )
            query_low = after(query_low, weights, weights_mine)
        activity = (depth_all > level).astype(jnp.int32)[:, None]
        attended, log_total = attend(places, low_key, activity, query_low, pairs)
        attended_low = attended.T
        attn_out = jnp.dot(attended_low, w_out, preferred_element_type=jnp.float32)
        mid_state = state + attn_out
        normed2, inverse2 = rms_forward(mid_state, norm2_gain)
        normed2_low = after(normed2.astype(jnp.bfloat16))
        gate_pre = low_dot(normed2_low, w_gate)
        up_pre = jnp.dot(normed2_low, w_up, preferred_element_type=jnp.float32)
        hidden_act = (jax.nn.silu(gate_pre.astype(jnp.float32)) * up_pre).astype(jnp.bfloat16)
        up_pre = up_pre.astype(jnp.bfloat16)
        ffn_out = jnp.dot(hidden_act, w_down, preferred_element_type=jnp.float32)
        gate_prob = jax.nn.sigmoid(
            jnp.dot(state, router_rows[level], precision=lax.Precision.HIGHEST)
        )
        active = (depth_row > level).astype(jnp.float32)
        both = attn_out + ffn_out
        saved.append(
            (
                state,
                inverse1,
                normed_low,
                query_low,
                pairs,
                activity,
                attended,
                log_total,
                attended_low,
                mid_state,
                inverse2,
                normed2_low,
                gate_pre,
                up_pre,
                hidden_act,
                both,
                gate_prob,
                active,
            )
        )
        state = state + (active * gate_prob)[:, None] * both
    mixed = state.astype(jnp.bfloat16)[None]
    grad_state = cotangent[0]
    normed2_all = stacked([item[11] for item in saved])
    hidden_all = stacked([item[14] for item in saved])
    rights = {kind: [None] * R for kind in ("down", "gate", "up", "out")}
    collected = None
    for level in range(R - 1, -1, -1):
        (
            state,
            inverse1,
            normed_low,
            query_low,
            pairs,
            activity,
            attended,
            log_total,
            attended_low,
            mid_state,
            inverse2,
            unused_low,
            gate_pre,
            up_pre,
            hidden_act,
            both,
            gate_prob,
            active,
        ) = saved[level]
        grad_branch = (active * gate_prob)[:, None] * grad_state
        grad_logit = jnp.sum(grad_state * both, axis=-1) * active * gate_prob * (1.0 - gate_prob)
        grad_next = grad_state + grad_logit[:, None] * router_rows[level][None, :]
        grad_ffn = grad_branch.astype(jnp.bfloat16)
        rights["down"][level] = low_dot(grad_ffn, spread_c)
        if level == 0:
            down_low, down_high = halves((down_left, stacked(rights["down"]), outer), 1)
            down_sent = added(value(down_high))
            down_got = swap(down_sent, 1)
            grad_ffn = after(grad_ffn, down_sent)
        grad_act = jnp.einsum("td,fd->tf", grad_ffn, w_down, preferred_element_type=jnp.float32)
        gate_pre, up_pre = (gate_pre.astype(jnp.float32), up_pre.astype(jnp.float32))
        sigma = jax.nn.sigmoid(gate_pre)
        grad_gate = (grad_act * up_pre * sigma * (1.0 + gate_pre * (1.0 - sigma))).astype(
            jnp.bfloat16
        )
        grad_up_pre = (grad_act * gate_pre * sigma).astype(jnp.bfloat16)
        rights["gate"][level] = grad_gate
        rights["up"][level] = grad_up_pre
        if level == 0:
            gate_low, gate_high = halves((gate_left, stacked(rights["gate"]), outer), 0)
            gate_sent = added(value(gate_high))
            gate_got = swap(gate_sent, 1)
            up_right = after(stacked(rights["up"]), gate_sent)
            up_low, up_high = halves((up_left, up_right, outer), 0)
            up_sent = added(value(up_high))
            up_got = swap(up_sent, 1)
            grad_gate, grad_up_pre = after((grad_gate, grad_up_pre), up_sent)
        grad_normed2 = jnp.einsum(
            "tf,df->td", grad_gate, w_gate, preferred_element_type=jnp.float32
        )
        grad_normed2 = grad_normed2 + jnp.einsum(
            "tf,df->td", grad_up_pre, w_up, preferred_element_type=jnp.float32
        )
        grad_mid, unused_gain = rms_backward(mid_state, inverse2, norm2_gain, grad_normed2)
        grad_next = grad_next + grad_mid
        grad_attn = (grad_branch + grad_mid).astype(jnp.bfloat16)
        spare = -width % 128
        rights["out"][level] = jnp.pad(grad_attn, ((0, 0), (0, spare)))
        if level == 0:
            out_low, out_high = halves((out_left, stacked(rights["out"]), outer), 0)
            out_sent = added(value(out_high))
            out_got = swap(out_sent, 1)

            def second(factors, got, stage, by_columns, mark):
                axis = axis_of(stage, by_columns)
                low, high = halves(factors, axis)
                got_low, got_high = [share_of(whole_of(got), axis, i, 2) for i in range(2)]
                left, right = after(high[:2], mark)
                send = added(high[2](left, right), part_of(got_high))
                return (send, low, got_low)

            gate_send, gate_low, gate_kept = second(gate_low, gate_got, order_a[0], False, out_sent)
            down_send, down_low, down_kept = second(
                down_low, down_got, order_c[0], True, gate_send
            )
            up_send, up_low, up_kept = second(up_low, up_got, order_b[0], False, down_send)
            out_send, out_low, out_kept = second(out_low, out_got, order_b[0], False, down_send)
            mix_send = jnp.concatenate([up_send, out_send], 1)
            gate_send, down_send, mix_send = after((gate_send, down_send, mix_send))
            gate_next = exchange(gate_send, order_a[0])
            down_next = exchange(down_send, order_c[0])
            mix_next = exchange(mix_send, order_b[0])
            grad_attn = after(grad_attn, gate_send, down_send, mix_send)
        grad_attended = jnp.einsum(
            "te,de->td", grad_attn, w_out, preferred_element_type=jnp.float32
        ).astype(jnp.bfloat16)
        grad_query, own_pair, prior = attend_back(
            places, low_key, activity, query_low, attended, grad_attended.T, log_total, pairs
        )
        prior = prior.reshape(REACH, -1, rows)
        two, mixed_pair, second_sum = halo_back(prior[0], prior[1], prior[2])
        if level == R - 1:
            attended_all, normed_all = after(
                (stacked([item[8] for item in saved]), stacked([item[2] for item in saved])),
                second_sum,
            )
            out_left = low_dot(attended_all, spread_b)
            front_left = low_dot(normed_all, spread_a)
        if level == R - 2:
            normed2_all, hidden_all = after((normed2_all, hidden_all), second_sum)
            gate_left = low_dot(normed2_all, spread_a)
            up_left = low_dot(normed2_all, spread_b)
            down_left = stream_order(hidden_all, order_c)
        if level == 0:

            def kept(factors, view, mark):
                left, right = after(factors[:2], mark)
                return added(factors[2](left, right), part_of(view))

            gate_base = kept(gate_low, gate_kept, prior)
            down_base = kept(down_low, down_kept, prior)
            mix_base = jnp.concatenate(
                [kept(up_low, up_kept, prior), kept(out_low, out_kept, prior)], 1
            )
            plan = {
                "gate": (order_a, False),
                "down": (order_c, True),
                "mix": (order_b, False),
                "front": (order_a, False),
            }
            views = {
                "gate": [whole_of(gate_base), whole_of(gate_next)],
                "down": [whole_of(down_base), whole_of(down_next)],
                "mix": [whole_of(mix_base), whole_of(mix_next)],
            }
            places_done = {"gate": 1, "down": 1, "mix": 1, "front": 0}

            groups = {kind: grouped(plan[kind][0]) for kind in plan}

            def step(kind, mark):
                group, by_columns = (groups[kind][places_done[kind]], plan[kind][1])
                sends, lows = to_send(views[kind], group, by_columns, mark)
                got = [exchange(send, mask_of(group, i + 1)) for i, send in enumerate(sends)]
                views[kind] = lows + [whole_of(block) for block in got]
                places_done[kind] += 1
                return tuple(sends)

            mark = (prior,)
            for kind in ("gate", "down", "mix"):
                mark = step(kind, mark)
            grad_query = after(grad_query, mark)
        collected, now = front(
            level,
            grad_query,
            own_pair.reshape(-1, rows),
            two,
            mixed_pair,
            cosine_tab,
            sine_tab,
            (grad_logit / inverse1[:, 0])[None, :],
            collected,
        )
        if level == 0:
            front_low, front_high = halves((front_left, collected, outer_t), 0)
            front_sent = added(value(front_high))
            front_got = swap(front_sent, 1)
            front_send, front_low, front_kept = second(
                front_low, front_got, order_a[0], False, mark
            )
            front_next = exchange(front_send, order_a[0])
            now = after(now, front_send)
            mark = front_send
            front_base = kept(front_low, front_kept, front_send)
            views["front"] = [whole_of(front_base), whole_of(front_next)]
            places_done["front"] = 1
        grad_normed = jnp.einsum("et,de->td", now, weights, preferred_element_type=jnp.float32)
        grad_input, unused_gain = rms_backward(state, inverse1, norm1_gain, grad_normed)
        grad_state = grad_next + grad_input
    kinds = ("gate", "down", "mix", "front")
    chain = kinds
    front_marks = [mark]
    while any(places_done[kind] < len(groups[kind]) for kind in kinds):
        for kind in chain:
            if places_done[kind] < len(groups[kind]):
                mark = step(kind, mark)
                front_marks = front_marks + [mark] if kind == "front" else front_marks
        chain = ("gate", "mix", "front")
        if all(places_done[kind] == len(groups[kind]) for kind in chain):
            while places_done["down"] < len(groups["down"]):
                step("down", front_marks[-2])
    for kind in ("gate", "mix"):
        arrays = after(tuple(view[0] for view in views[kind]), front_marks[-2])
        views[kind] = [(array,) + view[1:] for array, view in zip(arrays, views[kind])]
    parts = {kind: added(*[part_of(view) for view in views[kind]]) for kind in kinds}
    parts["mix"] = after(parts["mix"], front_marks[-1])
    parts["down"] = after(parts["down"], front_marks[-1])
    for kind in kinds:
        stages = [stage for stage in plan[kind][0] if stage[0] == "seq"]
        while stages:
            parts[kind] = widen_all(parts[kind], stages[-2:], plan[kind][1])
            stages = stages[:-2]
        parts[kind] = widen_all(parts[kind], [("seq", 1)], plan[kind][1])
    mix_part = parts["mix"]

    def finish(part, order):
        return jnp.dot(row_gather(width, order), part, preferred_element_type=jnp.float32)

    gate_sum = finish(parts["gate"], order_a)
    up_sum = finish(mix_part[:, : w_up.shape[1]], order_b)
    out_sum = finish(mix_part[:, w_up.shape[1] : w_up.shape[1] + width], order_b)
    front_sum = finish(parts["front"], order_a)
    down_sum = jnp.einsum(
        "fm,dm->fd", parts["down"], spread_c, preferred_element_type=jnp.float32
    )
    share = gate_sum.shape[0]
    first = lax.axis_index("str") * share

    def mine(table):
        return lax.dynamic_slice_in_dim(table, first, share, 0)

    gain1, gain2 = (mine(norm1_gain), mine(norm2_gain))
    first_key = width + -width % 128
    first_value = first_key + key_width + -key_width % 128
    query_sum = front_sum[:, :width]
    key_sum = front_sum[:, first_key : first_key + key_width]
    value_sum = front_sum[:, first_value : first_value + key_width]
    first_router = first_value + key_width
    router_sum = (front_sum[:, first_router : first_router + R] / gain1[:, None]).T

    def row_dots(weights, sums):
        return jnp.sum(mine(weights).astype(jnp.float32) * sums, axis=1)

    gain1_sum = jnp.sum(weights_mine.astype(jnp.float32) * front_sum, axis=1) / gain1
    gain2_sum = (row_dots(w_gate, gate_sum) + row_dots(w_up, up_sum)) / gain2
    return (
        mixed,
        grad_state[None],
        gain1_sum,
        query_sum,
        key_sum,
        value_sum,
        out_sum,
        gain2_sum,
        gate_sum,
        up_sum,
        down_sum,
        router_sum,
    )


def solution(mesh):
    in_specs = (
        P("str", "seq", None),
        P("str", None),
        P("str", "seq"),
        P("str", "seq", None),
        P(),
        P(),
        P(),
        P(),
        P(),
        P(),
        P(),
        P(),
        P(),
        P(),
    )
    out_specs = (
        P("str", "seq", None),
        P("str", "seq", None),
        P("str"),
        P("str", None),
        P("str", None),
        P("str", None),
        P("str", None),
        P("str"),
        P("str", None),
        P("str", None),
        P("str", None),
        P(None, "str"),
    )
    return jax.shard_map(
        per_device, mesh=mesh, in_specs=in_specs, out_specs=out_specs, check_vma=False
    )
```

```python
import functools
import math

import jax
import jax.numpy as jnp
from jax import lax
from jax.experimental import pallas as pl
from jax.experimental.pallas import tpu as pltpu
from jax.sharding import PartitionSpec as P

HD = 64
R = 3
REACH = 3


EPSILON = 1e-05


def rms_forward(values, gain):
    inverse = lax.rsqrt(jnp.mean(values * values, axis=-1, keepdims=True) + EPSILON)
    return (values * inverse * gain, inverse)


def rms_backward(values, inverse, gain, grad_out):
    scaled = grad_out * gain
    grad_gain = jnp.sum(grad_out * values * inverse, axis=0)
    grad_in = inverse * scaled - values * inverse * inverse * inverse * jnp.mean(
        scaled * values, axis=-1, keepdims=True
    )
    return (grad_in, grad_gain)


def rotate(values, cosine_tab, sine_tab):
    heads = values.reshape(-1, 2, HD // 2, values.shape[-1])
    first, second = (heads[:, 0], heads[:, 1])
    return jnp.stack(
        [first * cosine_tab - second * sine_tab, second * cosine_tab + first * sine_tab], 1
    ).reshape(values.shape)


def unrotate(grads, cosine_tab, sine_tab):
    return rotate(grads, cosine_tab, -sine_tab)


def doc_tables(positions, doc_lengths):
    ends = jnp.cumsum(doc_lengths, dtype=jnp.int32)
    after = positions[:, None] >= ends[None, :]
    doc_index = jnp.sum(after.astype(jnp.int32), axis=1, dtype=jnp.int32)
    offset = jnp.sum(jnp.where(after, doc_lengths[None, :], 0), axis=1, dtype=jnp.int32)
    return (doc_index, positions - offset)


def tile_bias(base, tile, low_key, positions, active):
    rows = active.shape[0]
    keys = base + tile * rows + lax.broadcasted_iota(jnp.int32, (rows, positions.shape[1]), 0)
    own = keys == positions
    seen = (keys >= low_key) & (keys <= positions) & ((active > 0) | own)
    return jnp.where(seen, 0.0, -1e30)


def gather_tiles(places, tiles, joined_ref):
    own, mixed, two, across = tiles
    rows = own.shape[1]
    even = places[2] == 0
    joined_ref[:, 3 * rows :] = own[...]
    joined_ref[:, 2 * rows : 3 * rows] = jnp.where(even, across[...], mixed[...])
    joined_ref[:, rows : 2 * rows] = two[...]
    joined_ref[:, :rows] = jnp.where(even, mixed[...], across[...])


def fill_bias(places, low_ref, act_ref, bias_ref):
    rows = bias_ref.shape[1]
    @pl.when(pl.program_id(0) == 0)
    def _():
        positions = places[0] + lax.broadcasted_iota(jnp.int32, (1, rows), 1)
        for tile in range(REACH + 1):
            part = slice(tile * rows, (tile + 1) * rows)
            bias_ref[part, :] = tile_bias(places[0] - REACH * rows, tile, low_ref[...], positions,
                                          act_ref[part, :])


def attend_kernel(places, low_ref, act_ref, query_ref, k0, k1, k2, k3, v0, v1, v2, v3,
                  out_ref, log_ref, bias_ref, key_ref, value_ref):
    rows = k0.shape[1]
    heads = query_ref.shape[0] // HD
    fill_bias(places, low_ref, act_ref, bias_ref)
    gather_tiles(places, (k0, k1, k2, k3), key_ref)
    gather_tiles(places, (v0, v1, v2, v3), value_ref)
    keys, values = (key_ref[...].T, value_ref[...])
    for i in range(heads):
        query = query_ref[i * HD:(i + 1) * HD, :] * jnp.bfloat16(HD ** (-0.5))
        s = jnp.dot(keys, query, preferred_element_type=jnp.float32) + bias_ref[...]
        top = jnp.max(s, axis=0, keepdims=True)
        p = jnp.exp(s - top)
        total = jnp.sum(p, axis=0, keepdims=True)
        acc = jnp.dot(values, p.astype(jnp.bfloat16), preferred_element_type=jnp.float32)
        out_ref[i * HD:(i + 1) * HD, :] = (acc / total).astype(jnp.bfloat16)
        log_ref[0, :, i * rows:(i + 1) * rows] = top + jnp.log(total)


def pair_specs(rows, heads):
    keys = pl.BlockSpec((HD, rows), lambda h, places: (h, 0))
    values = pl.BlockSpec((HD, rows), lambda h, places: (heads + h, 0))
    return [keys] * 4 + [values] * 4


def attend(places, low_key, active, query, pairs):
    width, rows = query.shape
    heads = pairs[0].shape[0] // (2 * HD)
    group = width // heads
    wide = group // HD * rows
    whole = lambda h, places: (0, 0)
    return pl.pallas_call(
        attend_kernel,
        out_shape=(jax.ShapeDtypeStruct((width, rows), jnp.bfloat16),
                   jax.ShapeDtypeStruct((heads, 1, wide), jnp.float32)),
        grid_spec=pltpu.PrefetchScalarGridSpec(
            num_scalar_prefetch=1, grid=(heads,),
            in_specs=[pl.BlockSpec((1, rows), whole), pl.BlockSpec((4 * rows, 1), whole),
                      pl.BlockSpec((group, rows), lambda h, places: (h, 0))] + pair_specs(rows, heads),
            out_specs=(pl.BlockSpec((group, rows), lambda h, places: (h, 0)),
                       pl.BlockSpec((1, 1, wide), lambda h, places: (h, 0, 0))),
            scratch_shapes=[pltpu.VMEM(((REACH + 1) * rows, rows), jnp.float32),
                            pltpu.VMEM((HD, (REACH + 1) * rows), jnp.bfloat16),
                            pltpu.VMEM((HD, (REACH + 1) * rows), jnp.bfloat16)]),
        cost_estimate=pl.CostEstimate(flops=4 * width * rows * rows * 16, bytes_accessed=4 * width * rows * 2, transcendentals=0),
        compiler_params=pltpu.CompilerParams(vmem_limit_bytes=7 << 20),
        name="attend",
    )(places, low_key, active, query, *pairs, *pairs)


def attend_back_kernel(places, low_ref, act_ref, query_ref, out_ref, grad_ref, log_ref, k0, k1, k2, k3, v0, v1, v2, v3,
                       dq_ref, own_ref, prev_ref, bias_ref, key_ref, value_ref):
    rows = k0.shape[1]
    heads = query_ref.shape[0] // HD
    fill_bias(places, low_ref, act_ref, bias_ref)
    gather_tiles(places, (k0, k1, k2, k3), key_ref)
    gather_tiles(places, (v0, v1, v2, v3), value_ref)
    keys = key_ref[...]
    key_rows, value_rows = (keys.T, value_ref[...].T)
    grad_keys = grad_values = None
    for i in range(heads):
        head = slice(i * HD, (i + 1) * HD)
        query = query_ref[head, :] * jnp.bfloat16(HD ** (-0.5))
        grad = grad_ref[head, :]
        delta = jnp.sum(grad.astype(jnp.float32) * out_ref[head, :].astype(jnp.float32), axis=0, keepdims=True)
        logs = log_ref[0, :, i * rows:(i + 1) * rows]
        p = jnp.exp(jnp.dot(key_rows, query, preferred_element_type=jnp.float32) + bias_ref[...] - logs)
        dp = jnp.dot(value_rows, grad, preferred_element_type=jnp.float32)
        ds = (p * (dp - delta)).astype(jnp.bfloat16)
        dq_ref[head, :] = jnp.dot(keys, ds, preferred_element_type=jnp.float32) * (HD ** (-0.5))
        dk = lax.dot_general(query, ds, (((1,), (1,)), ((), ())), preferred_element_type=jnp.float32)
        dv = lax.dot_general(grad, p.astype(jnp.bfloat16), (((1,), (1,)), ((), ())), preferred_element_type=jnp.float32)
        grad_keys = dk if i == 0 else grad_keys + dk
        grad_values = dv if i == 0 else grad_values + dv
    even = places[2] == 0
    own_ref[0] = grad_keys[:, REACH * rows:]
    own_ref[1] = grad_values[:, REACH * rows:]
    for tile in range(REACH):
        slot = jnp.where(even, tile, REACH - 1 - tile)
        part = slice(tile * rows, (tile + 1) * rows)
        prev_ref[slot, 0] = grad_keys[:, part].astype(jnp.bfloat16)
        prev_ref[slot, 1] = grad_values[:, part].astype(jnp.bfloat16)


def attend_back(places, low_key, active, query, out, grad, logs, pairs):
    width, rows = query.shape
    heads = pairs[0].shape[0] // (2 * HD)
    group = width // heads
    wide = group // HD * rows
    whole = lambda h, places: (0, 0)
    mine = pl.BlockSpec((group, rows), lambda h, places: (h, 0))
    own = pl.BlockSpec((2, HD, rows), lambda h, places: (0, h, 0))
    prev = pl.BlockSpec((REACH, 2, HD, rows), lambda h, places: (0, 0, h, 0))
    return pl.pallas_call(
        attend_back_kernel,
        out_shape=(jax.ShapeDtypeStruct((width, rows), jnp.float32),
                   jax.ShapeDtypeStruct((2, heads * HD, rows), jnp.float32),
                   jax.ShapeDtypeStruct((REACH, 2, heads * HD, rows), jnp.bfloat16)),
        grid_spec=pltpu.PrefetchScalarGridSpec(
            num_scalar_prefetch=1, grid=(heads,),
            in_specs=[pl.BlockSpec((1, rows), whole), pl.BlockSpec((4 * rows, 1), whole),
                      mine, mine, mine, pl.BlockSpec((1, 1, wide), lambda h, places: (h, 0, 0))] + pair_specs(rows, heads),
            out_specs=(mine, own, prev),
            scratch_shapes=[pltpu.VMEM(((REACH + 1) * rows, rows), jnp.float32),
                            pltpu.VMEM((HD, (REACH + 1) * rows), jnp.bfloat16),
                            pltpu.VMEM((HD, (REACH + 1) * rows), jnp.bfloat16)]),
        cost_estimate=pl.CostEstimate(flops=10 * width * rows * rows * 16, bytes_accessed=8 * width * rows * 2, transcendentals=0),
        compiler_params=pltpu.CompilerParams(vmem_limit_bytes=10 << 20),
        name="attend_back",
    )(places, low_key, active, query, out, grad, logs, *pairs, *pairs)


def front_kernel(level, query_ref, own_ref, two_ref, mixed_ref, cos_ref, sin_ref, router_ref, *refs):
    all_ref, now_ref = refs[-2:]
    width = query_ref.shape[0]
    half = HD // 2
    pair = own_ref[...] + two_ref[...].astype(jnp.float32) + mixed_ref[...].astype(jnp.float32)
    key_width = pair.shape[0] // 2
    cosine, sine = (cos_ref[...], sin_ref[...])
    turned = []
    for values in (query_ref[...], pair[:key_width]):
        for head in range(values.shape[0] // HD):
            first = values[head * HD : head * HD + half]
            second = values[head * HD + half : (head + 1) * HD]
            turned.append(first * cosine + second * sine)
            turned.append(second * cosine - first * sine)
    rows = pair.shape[1]
    blank = lambda size: jnp.zeros((-size % 128, rows), jnp.float32)
    place = lax.broadcasted_iota(jnp.int32, (-key_width % 128, rows), 0)
    cut = 2 * (width // HD)
    done = jnp.concatenate(
        turned[:cut]
        + [blank(width)]
        + turned[cut:]
        + [blank(key_width), pair[key_width:], jnp.where(place == level, router_ref[...], 0.0)],
        0,
    ).astype(jnp.bfloat16)
    now_ref[...] = done
    all_ref[...] = done


def front(level, query, own, two, mixed, cosine, sine, router_row, collected):
    width, rows = query.shape
    key_width = own.shape[0] // 2
    tall = width + -width % 128 + 2 * (key_width + -key_width % 128)
    block = pl.BlockSpec((tall, rows), lambda i: (0, level))
    inputs = [query, own, two, mixed, cosine, sine, router_row]
    specs = [pl.BlockSpec(item.shape, lambda i: (0, 0)) for item in inputs]
    aliases = {}
    if collected is not None:
        inputs.append(collected)
        specs.append(pl.BlockSpec(memory_space=pl.ANY))
        aliases = {len(inputs) - 1: 0}
    return pl.pallas_call(
        functools.partial(front_kernel, level),
        grid=(1,),
        out_shape=(
            jax.ShapeDtypeStruct((tall, R * rows), jnp.bfloat16),
            jax.ShapeDtypeStruct((tall, rows), jnp.bfloat16),
        ),
        in_specs=specs,
        out_specs=(block, pl.BlockSpec((tall, rows), lambda i: (0, 0))),
        input_output_aliases=aliases,
        compiler_params=pltpu.CompilerParams(vmem_limit_bytes=7 << 20),
        name="front",
    )(*inputs)


def swap(block, mask):
    devices = range(lax.axis_size("seq"))
    return lax.ppermute(block, "seq", [(i, i ^ mask) for i in devices])


def moved(block, targets):
    devices = range(lax.axis_size("seq"))
    return lax.ppermute(
        block, "seq", [(i, t) for i, t in enumerate(targets) if t in devices]
    )


def halo(block):
    devices = range(lax.axis_size("seq"))
    two = moved(block, [i + 2 for i in devices])
    mixed = moved(block, [i + 1 if i % 2 == 0 else i + 3 for i in devices])
    return (mixed, two, swap(two, 1))


def halo_back(mixed, second, across):
    devices = range(lax.axis_size("seq"))
    across = swap(across, 1)
    mixed = moved(mixed, [i - 1 if i % 2 == 1 else i - 3 for i in devices])
    second = added(second, across)
    two = moved(second, [i - 2 for i in devices])
    return (two, mixed, second)


def stage_lists():
    devices, streams = (lax.axis_size("seq"), lax.axis_size("str"))
    rest = [("seq", 1 << b) for b in range(1, devices.bit_length() - 1)]
    half = len(rest) // 2
    streams_bits = [("str", (2 << b) - 1) for b in range(streams.bit_length() - 1)]
    x_bits, y_bits = (rest[:half], rest[half:])
    return (
        x_bits + y_bits + streams_bits,
        y_bits + x_bits + streams_bits,
        streams_bits[:1] + y_bits + x_bits + streams_bits[1:],
    )


def exchange(block, stage):
    axis, mask = stage
    devices = range(lax.axis_size(axis))
    return lax.ppermute(block, axis, [(i, i ^ mask) for i in devices])


def offsets(index, stages):
    piece, stream = (index * 0, index * 0)
    for place, (axis, mask) in enumerate(reversed(stages)):
        bit = (index >> place) & 1
        if axis == "seq":
            piece = piece ^ (bit * mask)
        else:
            stream = stream ^ (bit * mask)
    return (piece, stream)


def slot_rows(width):
    devices, streams = (lax.axis_size("seq"), lax.axis_size("str"))
    share = width // streams
    slots = -(-share // devices)
    return (share, -(-slots // 8) * 8)


def one_hot(rows, columns):
    return (rows[:, None] == columns[None, :]).astype(jnp.bfloat16)


def row_spread(width, stages):
    devices, streams = (lax.axis_size("seq"), lax.axis_size("str"))
    share, slots = slot_rows(width)
    index = jnp.arange(devices * streams * slots, dtype=jnp.int32)
    piece, stream = offsets(index // slots, [("seq", 1)] + stages)
    inside = (piece ^ lax.axis_index("seq")) * slots + index % slots
    first = (stream ^ lax.axis_index("str")) * share
    target = jnp.where(inside < share, first + inside, -1)
    return one_hot(jnp.arange(width, dtype=jnp.int32), target)


def seq_only(stages):
    return [("seq", 1)] + [stage for stage in stages if stage[0] == "seq"]


def row_gather(width, stages):
    devices = lax.axis_size("seq")
    share, slots = slot_rows(width)
    index = jnp.arange(devices * slots, dtype=jnp.int32)
    piece, unused_stream = offsets(index // slots, seq_only(stages))
    target = (piece ^ lax.axis_index("seq")) * slots + index % slots
    return one_hot(jnp.arange(share, dtype=jnp.int32), target)


def column_spread(width, stages):
    devices = lax.axis_size("seq")
    used = -(-width // devices)
    lanes = -(-used // 128) * 128
    index = jnp.arange(devices * lanes, dtype=jnp.int32)
    piece, unused_stream = offsets(index // lanes, seq_only(stages))
    slot = index % lanes
    target = jnp.where(slot < used, (piece ^ lax.axis_index("seq")) * used + slot, -1)
    return one_hot(jnp.arange(width, dtype=jnp.int32), target)


def stream_order(values, stages):
    streams = lax.axis_size("str")
    size = values.shape[1] // streams
    bits = [stage for stage in stages if stage[0] == "str"]
    parts = []
    for index in range(streams):
        unused_piece, stream = offsets(index, bits)
        first = (lax.axis_index("str") ^ stream) * size
        parts.append(lax.dynamic_slice_in_dim(values, first, size, 1))
    return jnp.concatenate(parts, 1)


def low_dot(left, right):
    return jnp.dot(left, right, preferred_element_type=jnp.float32).astype(jnp.bfloat16)


def outer(left, right):
    return jnp.einsum("tm,tn->mn", left, right, preferred_element_type=jnp.float32)


def outer_t(left, right):
    return jnp.einsum("tm,nt->mn", left, right, preferred_element_type=jnp.float32)


def added(*terms):
    total = terms[0].astype(jnp.float32)
    for term in terms[1:]:
        total = total + term.astype(jnp.float32)
    return total.astype(jnp.bfloat16)


def after(values, *marks):
    held = lax.optimization_barrier((values, marks))
    return held[0]


def axis_of(stage, by_columns):
    return 1 if by_columns and stage[0] == "seq" else 0


def halves(factors, axis):
    left, right, product = factors
    if axis == 0:
        half = left.shape[1] // 2
        return ((left[:, :half], right, product), (left[:, half:], right, product))
    half = right.shape[1] // 2
    return ((left, right[:, :half], product), (left, right[:, half:], product))


def value(factors):
    left, right, product = factors
    return product(left, right)


def share_of(view, axis, place, parts):
    array, row, column, rows, columns = view
    if axis == 0:
        rows = rows // parts
        return (array, row + place * rows, column, rows, columns)
    columns = columns // parts
    return (array, row, column + place * columns, rows, columns)


def grouped(stages):
    groups = []
    for stage in stages:
        if stage[0] == "str" and groups and groups[-1][0][0] == "str" and len(groups[-1]) < 2:
            groups[-1].append(stage)
        else:
            groups.append([stage])
    return groups


def mask_of(group, place):
    mask = 0
    for bit, stage in enumerate(reversed(group)):
        if (place >> bit) & 1:
            mask ^= stage[1]
    return (group[0][0], mask)


def whole_of(array):
    return (array, 0, 0, array.shape[0], array.shape[1])


def part_of(view):
    array, row, column, rows, columns = view
    return lax.slice(array, (row, column), (row + rows, column + columns))


def to_send(views, group, by_columns, mark):
    axis = axis_of(group[0], by_columns)
    parts = 1 << len(group)
    arrays = after(tuple(view[0] for view in views), mark)
    held = [(array,) + view[1:] for array, view in zip(arrays, views)]
    sends = [
        added(*[part_of(share_of(view, axis, place, parts)) for view in held])
        for place in range(1, parts)
    ]
    return (sends, [share_of(view, axis, 0, parts) for view in views])


def second(factors, got, stage, by_columns, mark):
    axis = axis_of(stage, by_columns)
    low, high = halves(factors, axis)
    got_low, got_high = [share_of(whole_of(got), axis, i, 2) for i in range(2)]
    left, right = after(high[:2], mark)
    send = added(high[2](left, right), part_of(got_high))
    return (send, low, got_low)


def widen_all(part, group, by_columns=False):
    pieces = [part] + [exchange(part, mask_of(group, i)) for i in range(1, 1 << len(group))]
    return jnp.concatenate(pieces, 1 if by_columns else 0)


def stacked(values):
    return jnp.concatenate(values, 0)


def per_device(
    hidden,
    lengths,
    depth,
    cotangent,
    norm1_gain,
    w_query,
    w_key,
    w_value,
    w_out,
    norm2_gain,
    w_gate,
    w_up,
    w_down,
    router,
):
    rows, width = hidden.shape[1:]
    key_width = w_key.shape[1]
    seq_index = lax.axis_index("seq")
    local_pos = seq_index * rows + jnp.arange(rows, dtype=jnp.int32)
    doc_lengths = lengths[0]
    unused_doc, place = doc_tables(local_pos, doc_lengths)
    low_key = (local_pos - place)[None, :]
    window = (seq_index - REACH) * rows
    first_tile = jnp.maximum((low_key[0, 0] - window) // rows, 0)
    even = seq_index % 2
    places = jnp.stack([seq_index * rows, first_tile, even]).astype(jnp.int32)
    half = HD // 2
    freqs = jnp.exp(-math.log(10000.0) * 2.0 * jnp.arange(half, dtype=jnp.float32) / HD)
    angles = freqs[:, None] * place.astype(jnp.float32)[None, :]
    cosine_tab = jnp.cos(angles)
    sine_tab = jnp.sin(angles)
    depth_row = depth[0]
    mixed_depth, two_depth, across_depth = halo(depth_row)
    depth_all = jnp.concatenate(
        [
            jnp.where(even == 0, mixed_depth, across_depth),
            two_depth,
            jnp.where(even == 0, across_depth, mixed_depth),
            depth_row,
        ],
        0,
    )
    router_rows = router.astype(jnp.float32)
    order_a, order_b, order_c = stage_lists()
    spread_a = row_spread(width, order_a)
    spread_b = row_spread(width, order_b)
    spread_c = column_spread(width, order_c)
    state = hidden[0].astype(jnp.float32)
    saved = []
    for level in range(R):
        normed, inverse1 = rms_forward(state, norm1_gain)
        normed_low = normed.astype(jnp.bfloat16)
        key_pre = jnp.dot(normed_low, w_key, preferred_element_type=jnp.float32)
        value_low = low_dot(normed_low, w_value)
        key_low = rotate(key_pre.T, cosine_tab, sine_tab).astype(jnp.bfloat16)
        local_pair = jnp.concatenate([key_low, value_low.T], 0)
        pairs = (local_pair, *halo(local_pair))
        query_pre = jnp.dot(normed_low, w_query, preferred_element_type=jnp.float32)
        query_low = rotate(query_pre.T, cosine_tab, sine_tab).astype(jnp.bfloat16)
        if level == 1:
            weights = jnp.concatenate(
                [
                    jnp.pad(item, ((0, 0), (0, -item.shape[1] % 128)))
                    for item in after((w_query, w_key, w_value), local_pair)
                ],
                1,
            )
            share = width // lax.axis_size("str")
            weights_mine = lax.dynamic_slice_in_dim(
                weights, lax.axis_index("str") * share, share, 0
            )
            query_low = after(query_low, weights, weights_mine)
        activity = (depth_all > level).astype(jnp.int32)[:, None]
        attended, log_total = attend(places, low_key, activity, query_low, pairs)
        attended_low = attended.T
        attn_out = jnp.dot(attended_low, w_out, preferred_element_type=jnp.float32)
        mid_state = state + attn_out
        normed2, inverse2 = rms_forward(mid_state, norm2_gain)
        normed2_low = after(normed2.astype(jnp.bfloat16))
        gate_pre = low_dot(normed2_low, w_gate)
        up_pre = jnp.dot(normed2_low, w_up, preferred_element_type=jnp.float32)
        hidden_act = (jax.nn.silu(gate_pre.astype(jnp.float32)) * up_pre).astype(jnp.bfloat16)
        up_pre = up_pre.astype(jnp.bfloat16)
        ffn_out = jnp.dot(hidden_act, w_down, preferred_element_type=jnp.float32)
        gate_prob = jax.nn.sigmoid(
            jnp.dot(state, router_rows[level], precision=lax.Precision.HIGHEST)
        )
        active = (depth_row > level).astype(jnp.float32)
        both = attn_out + ffn_out
        saved.append(
            (
                state,
                inverse1,
                normed_low,
                query_low,
                pairs,
                activity,
                attended,
                log_total,
                attended_low,
                mid_state,
                inverse2,
                normed2_low,
                gate_pre,
                up_pre,
                hidden_act,
                both,
                gate_prob,
                active,
            )
        )
        state = state + (active * gate_prob)[:, None] * both
    mixed = state.astype(jnp.bfloat16)[None]
    grad_state = cotangent[0]
    normed2_all = stacked([item[11] for item in saved])
    hidden_all = stacked([item[14] for item in saved])
    rights = {kind: [None] * R for kind in ("down", "gate", "up", "out")}
    collected = None
    for level in range(R - 1, -1, -1):
        (
            state,
            inverse1,
            normed_low,
            query_low,
            pairs,
            activity,
            attended,
            log_total,
            attended_low,
            mid_state,
            inverse2,
            unused_low,
            gate_pre,
            up_pre,
            hidden_act,
            both,
            gate_prob,
            active,
        ) = saved[level]
        grad_branch = (active * gate_prob)[:, None] * grad_state
        grad_logit = jnp.sum(grad_state * both, axis=-1) * active * gate_prob * (1.0 - gate_prob)
        grad_next = grad_state + grad_logit[:, None] * router_rows[level][None, :]
        grad_ffn = grad_branch.astype(jnp.bfloat16)
        rights["down"][level] = low_dot(grad_ffn, spread_c)
        if level == 0:
            down_low, down_high = halves((down_left, stacked(rights["down"]), outer), 1)
            down_sent = added(value(down_high))
            down_got = swap(down_sent, 1)
            grad_ffn = after(grad_ffn, down_sent)
        grad_act = jnp.einsum("td,fd->tf", grad_ffn, w_down, preferred_element_type=jnp.float32)
        gate_pre, up_pre = (gate_pre.astype(jnp.float32), up_pre.astype(jnp.float32))
        sigma = jax.nn.sigmoid(gate_pre)
        grad_gate = (grad_act * up_pre * sigma * (1.0 + gate_pre * (1.0 - sigma))).astype(
            jnp.bfloat16
        )
        grad_up_pre = (grad_act * gate_pre * sigma).astype(jnp.bfloat16)
        rights["gate"][level] = grad_gate
        rights["up"][level] = grad_up_pre
        if level == 0:
            gate_low, gate_high = halves((gate_left, stacked(rights["gate"]), outer), 0)
            gate_sent = added(value(gate_high))
            gate_got = swap(gate_sent, 1)
            down_send, down_low, down_kept = second(
                down_low, down_got, order_c[0], True, gate_sent
            )
            down_next = exchange(down_send, order_c[0])
            up_right = after(stacked(rights["up"]), down_send)
            up_low, up_high = halves((up_left, up_right, outer), 0)
            up_sent = added(value(up_high))
            up_got = swap(up_sent, 1)
            gate_send, gate_low, gate_kept = second(
                gate_low, gate_got, order_a[0], False, up_sent
            )
            gate_next = exchange(gate_send, order_a[0])
            up_send, up_low, up_kept = second(up_low, up_got, order_b[0], False, gate_send)
            up_next = exchange(up_send, order_b[0])
            grad_gate, grad_up_pre = after((grad_gate, grad_up_pre), up_send)
        grad_normed2 = jnp.einsum(
            "tf,df->td", grad_gate, w_gate, preferred_element_type=jnp.float32
        )
        grad_normed2 = grad_normed2 + jnp.einsum(
            "tf,df->td", grad_up_pre, w_up, preferred_element_type=jnp.float32
        )
        grad_mid, unused_gain = rms_backward(mid_state, inverse2, norm2_gain, grad_normed2)
        grad_next = grad_next + grad_mid
        grad_attn = (grad_branch + grad_mid).astype(jnp.bfloat16)
        spare = -width % 128
        rights["out"][level] = jnp.pad(grad_attn, ((0, 0), (0, spare)))
        if level == 0:
            out_low, out_high = halves((out_left, stacked(rights["out"]), outer), 0)
            out_sent = added(value(out_high))
            out_got = swap(out_sent, 1)

            out_send, out_low, out_kept = second(out_low, out_got, order_b[0], False, out_sent)
            out_next = exchange(out_send, order_b[0])
            mix_next = jnp.concatenate([up_next, out_next], 1)
            grad_attn = after(grad_attn, gate_send, down_send, up_send, out_send)
        grad_attended = jnp.einsum(
            "te,de->td", grad_attn, w_out, preferred_element_type=jnp.float32
        ).astype(jnp.bfloat16)
        grad_query, own_pair, prior = attend_back(
            places, low_key, activity, query_low, attended, grad_attended.T, log_total, pairs
        )
        prior = prior.reshape(REACH, -1, rows)
        two, mixed_pair, second_sum = halo_back(prior[0], prior[1], prior[2])
        if level == R - 1:
            attended_all, normed_all = after(
                (stacked([item[8] for item in saved]), stacked([item[2] for item in saved])),
                second_sum,
            )
            out_left = low_dot(attended_all, spread_b)
            front_left = low_dot(normed_all, spread_a)
            two = after(two, out_left, front_left)
        if level == R - 2:
            normed2_all, hidden_all = after((normed2_all, hidden_all), second_sum)
            gate_left = low_dot(normed2_all, spread_a)
            up_left = low_dot(normed2_all, spread_b)
            down_left = stream_order(hidden_all, order_c)
            two = after(two, gate_left, up_left, down_left)
        if level == 0:

            def kept(factors, view, mark):
                left, right = after(factors[:2], mark)
                return added(factors[2](left, right), part_of(view))

            gate_base = kept(gate_low, gate_kept, prior)
            down_base = kept(down_low, down_kept, prior)
            mix_base = jnp.concatenate(
                [kept(up_low, up_kept, prior), kept(out_low, out_kept, prior)], 1
            )
            plan = {
                "gate": (order_a, False),
                "down": (order_c, True),
                "mix": (order_b, False),
                "front": (order_a, False),
            }
            views = {
                "gate": [whole_of(gate_base), whole_of(gate_next)],
                "down": [whole_of(down_base), whole_of(down_next)],
                "mix": [whole_of(mix_base), whole_of(mix_next)],
            }
            places_done = {"gate": 1, "down": 1, "mix": 1, "front": 0}

            groups = {kind: grouped(plan[kind][0]) for kind in plan}

            def step(kind, mark):
                group, by_columns = (groups[kind][places_done[kind]], plan[kind][1])
                sends, lows = to_send(views[kind], group, by_columns, mark)
                got = [exchange(send, mask_of(group, i + 1)) for i, send in enumerate(sends)]
                views[kind] = lows + [whole_of(block) for block in got]
                places_done[kind] += 1
                return tuple(sends)

            mark = (prior,)
            for kind in ("gate", "down", "mix"):
                mark = step(kind, mark)
            grad_query = after(grad_query, mark)
        collected, now = front(
            level,
            grad_query,
            own_pair.reshape(-1, rows),
            two,
            mixed_pair,
            cosine_tab,
            sine_tab,
            (grad_logit / inverse1[:, 0])[None, :],
            collected,
        )
        if level == 0:
            front_low, front_high = halves((front_left, collected, outer_t), 0)
            front_sent = added(value(front_high))
            front_got = swap(front_sent, 1)
            front_send, front_low, front_kept = second(
                front_low, front_got, order_a[0], False, mark
            )
            front_next = exchange(front_send, order_a[0])
            now = after(now, front_send)
            mark = front_send
            front_base = kept(front_low, front_kept, front_send)
            views["front"] = [whole_of(front_base), whole_of(front_next)]
            places_done["front"] = 1
        grad_normed = jnp.einsum("et,de->td", now, weights, preferred_element_type=jnp.float32)
        grad_input, unused_gain = rms_backward(state, inverse1, norm1_gain, grad_normed)
        grad_state = grad_next + grad_input
    kinds = ("gate", "down", "mix", "front")
    chain = kinds
    front_marks = [mark]
    while any(places_done[kind] < len(groups[kind]) for kind in kinds):
        for kind in chain:
            if places_done[kind] < len(groups[kind]):
                mark = step(kind, mark)
                front_marks = front_marks + [mark] if kind == "front" else front_marks
        chain = ("gate", "mix", "front")
        if all(places_done[kind] == len(groups[kind]) for kind in chain):
            while places_done["down"] < len(groups["down"]):
                step("down", front_marks[-2])
    for kind in ("gate", "mix"):
        arrays = after(tuple(view[0] for view in views[kind]), front_marks[-2])
        views[kind] = [(array,) + view[1:] for array, view in zip(arrays, views[kind])]
    parts = {kind: added(*[part_of(view) for view in views[kind]]) for kind in kinds}
    parts["mix"] = after(parts["mix"], front_marks[-1])
    parts["down"] = after(parts["down"], front_marks[-1])
    for kind in kinds:
        stages = [stage for stage in plan[kind][0] if stage[0] == "seq"]
        while stages:
            parts[kind] = widen_all(parts[kind], stages[-2:], plan[kind][1])
            stages = stages[:-2]
        if kind == "front":
            gate_sum = jnp.dot(
                row_gather(width, order_a), parts["gate"], preferred_element_type=jnp.float32
            )
            share = gate_sum.shape[0]
            gate_dots = jnp.sum(
                lax.dynamic_slice_in_dim(
                    w_gate, lax.axis_index("str") * share, share, 0
                ).astype(jnp.float32)
                * gate_sum,
                axis=1,
            )
            parts[kind] = after(parts[kind], gate_sum, gate_dots)
        parts[kind] = widen_all(parts[kind], [("seq", 1)], plan[kind][1])
    mix_part = parts["mix"]

    def finish(part, order):
        return jnp.dot(row_gather(width, order), part, preferred_element_type=jnp.float32)

    up_sum = finish(mix_part[:, : w_up.shape[1]], order_b)
    out_sum = finish(mix_part[:, w_up.shape[1] : w_up.shape[1] + width], order_b)
    front_sum = finish(parts["front"], order_a)
    down_sum = jnp.einsum(
        "fm,dm->fd", parts["down"], spread_c, preferred_element_type=jnp.float32
    )
    share = gate_sum.shape[0]
    first = lax.axis_index("str") * share

    def mine(table):
        return lax.dynamic_slice_in_dim(table, first, share, 0)

    gain1, gain2 = (mine(norm1_gain), mine(norm2_gain))
    first_key = width + -width % 128
    first_value = first_key + key_width + -key_width % 128
    query_sum = front_sum[:, :width]
    key_sum = front_sum[:, first_key : first_key + key_width]
    value_sum = front_sum[:, first_value : first_value + key_width]
    first_router = first_value + key_width
    router_sum = (front_sum[:, first_router : first_router + R] / gain1[:, None]).T

    def row_dots(weights, sums):
        return jnp.sum(mine(weights).astype(jnp.float32) * sums, axis=1)

    gain1_sum = jnp.sum(weights_mine.astype(jnp.float32) * front_sum, axis=1) / gain1
    gain2_sum = (gate_dots + row_dots(w_up, up_sum)) / gain2
    return (
        mixed,
        grad_state[None],
        gain1_sum,
        query_sum,
        key_sum,
        value_sum,
        out_sum,
        gain2_sum,
        gate_sum,
        up_sum,
        down_sum,
        router_sum,
    )


def solution(mesh):
    in_specs = (
        P("str", "seq", None),
        P("str", None),
        P("str", "seq"),
        P("str", "seq", None),
        P(),
        P(),
        P(),
        P(),
        P(),
        P(),
        P(),
        P(),
        P(),
        P(),
    )
    out_specs = (
        P("str", "seq", None),
        P("str", "seq", None),
        P("str"),
        P("str", None),
        P("str", None),
        P("str", None),
        P("str", None),
        P("str"),
        P("str", None),
        P("str", None),
        P("str", None),
        P(None, "str"),
    )
    return jax.shard_map(
        per_device, mesh=mesh, in_specs=in_specs, out_specs=out_specs, check_vma=False
    )
```
